512 devices in a mesh: ctx: 128 (over z, x_hi, y), fsdp: 4 (over x_lo, core).
Axes of the slice: x: 4 (x_hi: 2, x_lo: 2; x = x_hi * 2 + x_lo), y: 4, z: 16, core: 2. Of those that a mesh axis runs over, the one named last changes fastest.
Arguments:
- normed: bfloat16 [2, 4, 16384, 1024], P(None, 'fsdp', 'ctx'), may hold values from -6 to 6
- out_grad: bfloat16 [2, 4, 16384, 1024], P(None, 'fsdp', 'ctx'), may hold values from -6 to 6
- ids: int32 [2, 4, 16384], P(None, 'fsdp', 'ctx'), may hold values from 0 to 4, as said below
- mask: int32 [2, 4, 16384], P(None, 'fsdp', 'ctx'), may hold values 0 or 1
- proj_half: bfloat16 [512, 1024], P('fsdp'), may hold values from -0.1875 to 0.1875
- conv_filter: float32 [7, 1024], replicated, may hold values from -2.5 to 2.5
- gate_bias: float32 [6, 1024], replicated, may hold values from -6 to 6
Outputs:
- in_grad: bfloat16 [2, 4, 16384, 1024], P(None, 'fsdp', 'ctx')
- proj_grad: float32 [128, 512, 1024], P('ctx', 'fsdp')
- filter_grad: float32 [128, 7, 1024], P('ctx', None, 'fsdp')
- bias_grad: float32 [128, 6, 1024], P('ctx', None, 'fsdp')
The draws below stay inside these ranges and needn't reach their ends.
Inputs may be any that keep to these rules, and one draw needn't show every extreme that they name: Codes A=0, C=1, G=2, T=3, N=4. ids[1] is the reverse complement of ids[0] in its own coordinates: ids[1, b, p] = 3 - ids[0, b, 16383 - p] where that code is below 4, and 4 where it is 4. Every sequence holds at least one 4.
All inputs are finite; a program needn't handle non-finite values. No bound on the sum of `mask` on one device may be relied on, other than what follows from the above.
Results may differ from the reference program's by a relative error of at most 0.007.
Values may be sent and summed in bfloat16 or wider, within the bound.
No kernel may reach another device: no remote copies, remote signals or barrier semaphores. Data moves between devices by JAX's collectives and lax.ppermute only.
A program may use at most 64 MiB of HBM per device.

```python
import math
import jax
import jax.numpy as jnp
from jax import lax

D = 1024
K = 7
ROWS = 128
SEQ = 16384
BATCH = 4
N_CTX = 128


def draw_ids(key, part):
    base_ids = jax.random.randint(jax.random.fold_in(key, 11), (BATCH, SEQ), 0, 4, dtype=jnp.int32)
    unknown = jax.random.randint(jax.random.fold_in(key, 12), (BATCH, SEQ), 0, 64, dtype=jnp.int32) == 0
    forced = jax.random.randint(jax.random.fold_in(key, 13), (BATCH, 1), 0, SEQ, dtype=jnp.int32)
    at_forced = lax.broadcasted_iota(jnp.int32, (BATCH, SEQ), 1) == forced
    forward = jnp.where(unknown | at_forced, 4, base_ids)
    reverse = jnp.flip(jnp.where(forward == 4, 4, 3 - forward), axis=1)
    return jnp.stack([forward, reverse], axis=0)


def touch_ends(entries, key, least, high):
    longest = entries.shape.index(max(entries.shape))
    spots = []
    for shift in (0, 1):
        where = [jax.random.randint(jax.random.fold_in(key, axis), (), 0, length) for axis, length in enumerate(entries.shape)]
        where[longest] = (where[longest] + shift) % entries.shape[longest]
        spots.append(tuple(where))
    return entries.at[spots[0]].set(least).at[spots[1]].set(high)


def steps_of(rng, shape, shards, least, largest):
    def one(axis_at, parts):
        steps = jax.random.uniform(jax.random.fold_in(jax.random.fold_in(rng, 6), axis_at), (parts,), jnp.float32, least / len(shards), largest / len(shards))
        return jnp.repeat(jnp.exp(steps), shape[axis_at] // parts).reshape((-1,) + (1,) * (len(shape) - axis_at - 1))

    factor_of = one(*shards[0])
    for cut in shards[1:]:
        factor_of = factor_of * one(*cut)
    return factor_of


def bell_draw(stream_key, extent, deviation, limit, cuts=(), kind=jnp.bfloat16):
    array = jax.random.normal(stream_key, extent, jnp.float32) * deviation
    if len(cuts) > 0:
        array = steps_of(stream_key, extent, cuts, -0.22, 0.18) * array
    return jnp.clip(array, min=-limit, max=limit).astype(kind)


def setup_inputs(seed: int = 0) -> dict:
    splits = jax.random.split(jax.random.key(seed), 8)
    return {
        "normed": bell_draw(splits[0], (2, BATCH, SEQ, D), 1.0, 6.0, ((1, 4), (2, 128))),
        "out_grad": bell_draw(splits[1], (2, BATCH, SEQ, D), 1.0, 6.0, ((1, 4), (2, 128))),
        "ids": draw_ids(jax.random.fold_in(splits[7], 71), 0),
        "mask": touch_ends((jax.random.randint(splits[3], (2, BATCH, SEQ), 0, 20) < 3).astype(jnp.int32), jax.random.fold_in(splits[3], 1), 0, 1),
        "proj_half": bell_draw(splits[4], (D // 2, D), D ** -0.5, 0.1875, ((0, 4),)),
        "conv_filter": bell_draw(splits[5], (K, D), 0.4, 2.5, (), jnp.float32),
        "gate_bias": bell_draw(splits[6], (6, D), 1.0, 6.0, (), jnp.float32),
    }


def reference(normed, out_grad, ids, mask, proj_half, conv_filter, gate_bias):
    weight_full = jnp.concatenate([proj_half, jnp.flip(proj_half, axis=(0, 1))], axis=0)
    half_width = D // 2
    scale = 1.0 / math.sqrt(2.0 * BATCH * ROWS)

    def one_sequence(totals, pieces):
        seq_in, seq_grad, seq_ids, seq_mask = pieces
        flat_in = seq_in.reshape(-1, D)
        values = jnp.dot(flat_in, weight_full, preferred_element_type=jnp.float32).astype(jnp.bfloat16).reshape(2, SEQ, D)
        extended = jnp.pad(values, ((0, 0), (K - 1, 0), (0, 0)))
        conv_out = jnp.zeros((2, SEQ, D), jnp.float32)
        for tap_index in range(K):
            start_row = K - 1 - tap_index
            conv_out = conv_out + conv_filter[tap_index] * extended[:, start_row:start_row + SEQ, :].astype(jnp.float32)
        mirrored = jnp.flip(values, axis=(0, 1, 2))
        tokens = jnp.where(seq_mask == 1, 5, seq_ids)
        gate = jax.nn.sigmoid(mirrored.astype(jnp.float32) + gate_bias[tokens])
        cotangent = seq_grad.astype(jnp.float32)
        conv_grad = cotangent * gate
        gate_pre = cotangent * conv_out * gate * (1.0 - gate)
        mirror_grad = gate_pre.astype(jnp.bfloat16)
        grad_ext = jnp.pad(conv_grad, ((0, 0), (0, K - 1), (0, 0)))
        value_grad = jnp.flip(mirror_grad, axis=(0, 1, 2)).astype(jnp.float32)
        for tap_index in range(K):
            value_grad = value_grad + conv_filter[tap_index] * grad_ext[:, tap_index:tap_index + SEQ, :]
        value_grad = value_grad.astype(jnp.bfloat16)
        flat_grad = value_grad.reshape(-1, D)
        in_grad = jnp.dot(flat_grad, weight_full.T, preferred_element_type=jnp.float32).astype(jnp.bfloat16).reshape(2, SEQ, D)
        blocks_in = seq_in.reshape(2, N_CTX, ROWS, D).astype(jnp.float32)
        blocks_grad = value_grad.reshape(2, N_CTX, ROWS, D).astype(jnp.float32)
        proj_part = jnp.einsum('scrd,scre->cde', blocks_in[..., :half_width], blocks_grad, precision=lax.Precision.HIGHEST)
        proj_part = proj_part + jnp.einsum('scrd,scre->cde', jnp.flip(blocks_in[..., half_width:], axis=3), jnp.flip(blocks_grad, axis=3), precision=lax.Precision.HIGHEST)
        filter_terms = []
        for tap_index in range(K):
            start_row = K - 1 - tap_index
            product = conv_grad * extended[:, start_row:start_row + SEQ, :].astype(jnp.float32)
            filter_terms.append(lax.optimization_barrier(jnp.sum(product.reshape(2, N_CTX, ROWS, D), axis=(0, 2))))
        filter_part = jnp.stack(filter_terms, axis=1)
        classes = jnp.arange(6, dtype=jnp.int32)
        one_hot = (tokens[..., None] == classes).astype(jnp.float32)
        bias_part = jnp.einsum('scrt,scrd->ctd', one_hot.reshape(2, N_CTX, ROWS, 6), gate_pre.reshape(2, N_CTX, ROWS, D), precision=lax.Precision.HIGHEST)
        totals = (totals[0] + proj_part, totals[1] + filter_part, totals[2] + bias_part)
        return (totals, in_grad)
    start_totals = (jnp.zeros((N_CTX, D // 2, D), jnp.float32), jnp.zeros((N_CTX, K, D), jnp.float32), jnp.zeros((N_CTX, 6, D), jnp.float32))
    pieces = (jnp.moveaxis(normed, 1, 0), jnp.moveaxis(out_grad, 1, 0), jnp.moveaxis(ids, 1, 0), jnp.moveaxis(mask, 1, 0))
    totals, grads_in = lax.scan(one_sequence, start_totals, pieces)
    in_grad = jnp.moveaxis(grads_in, 0, 1)
    return (in_grad, totals[0] * scale, totals[1] * scale, totals[2] * scale)
```

```python
import functools
import math

import jax
import jax.numpy as jnp
from jax import lax
from jax.experimental import pallas as pl
from jax.experimental.pallas import tpu as pltpu
from jax.sharding import PartitionSpec as P

LANES = 128
HALO = 8
F32 = jnp.float32
BF16 = jnp.bfloat16
HIGHEST = lax.Precision.HIGHEST


def dot(a, b):
    return jnp.dot(a, b, preferred_element_type=F32)


def reversal(size, dtype=BF16):
    rows = lax.broadcasted_iota(jnp.int32, (size, size), 0)
    cols = lax.broadcasted_iota(jnp.int32, (size, size), 1)
    return (rows + cols == size - 1).astype(dtype)


def reverse_lanes(value, precision=None):
    count = value.shape[-1] // LANES
    swap = reversal(LANES, value.dtype)
    parts = []
    for block in reversed(range(count)):
        part = value[:, block * LANES : (block + 1) * LANES]
        parts.append(
            jnp.dot(part, swap, preferred_element_type=F32, precision=precision).astype(value.dtype)
        )
    return jnp.concatenate(parts, axis=1)


def reverse_rows(value):
    return dot(reversal(value.shape[0]), value).astype(value.dtype)


def reverse_both(value):
    return reverse_lanes(reverse_rows(value))


def call(kernel, out_shapes, *operands, scalars=0, scratch=(), flops=0, moved=0):
    specs = [pl.BlockSpec(memory_space=pltpu.SMEM)] * scalars
    specs += [pl.BlockSpec(memory_space=pltpu.VMEM)] * (len(operands) - scalars)
    return pl.pallas_call(
        kernel,
        out_shape=out_shapes,
        in_specs=specs,
        out_specs=[pl.BlockSpec(memory_space=pltpu.VMEM)] * len(out_shapes),
        scratch_shapes=list(scratch),
        cost_estimate=pl.CostEstimate(flops=flops, bytes_accessed=moved, transcendentals=0),
        compiler_params=pltpu.CompilerParams(vmem_limit_bytes=48 * 1024 * 1024),
    )(*operands)


def pack_kernel(grad_ref, tokens_ref, tail_ref, head_ref, slab_ref):
    rows = grad_ref.shape[0]
    head = head_ref[...].astype(F32)
    tail = tail_ref[...].astype(F32)
    tail_rev = jnp.dot(reversal(HALO, F32), tail, preferred_element_type=F32).astype(BF16)
    head_rev = jnp.dot(reversal(HALO, F32), head, preferred_element_type=F32).astype(BF16)
    near = head[HALO - 1 : HALO, :LANES].astype(BF16)
    own = tokens_ref[...].astype(F32).astype(BF16)
    both = jnp.concatenate([own, near, jnp.zeros((6, LANES), BF16)], axis=0)
    flipped = dot(both, reversal(LANES))
    token_row = jnp.concatenate(
        [flipped[0:1], flipped[1:2], jnp.zeros((1, slab_ref.shape[1] - 2 * LANES), F32)], axis=1
    )
    at_row = lax.broadcasted_iota(jnp.int32, (HALO, slab_ref.shape[1]), 0) == HALO - 1
    tail_out = jnp.where(at_row, token_row, reverse_lanes(tail_rev).astype(F32)).astype(BF16)
    slab_ref[0:HALO, :] = reverse_lanes(head_rev)
    slab_ref[HALO : HALO + rows, :] = reverse_both(grad_ref[...])
    slab_ref[HALO + rows :, :] = tail_out


def forward_kernel(place_ref, pair_ref, other_ref, normed_ref, tail_ref, weight_ref, values_ref):
    shard = pair_ref.shape[0] // 2
    half = 4 * shard
    x_lo = place_ref[0] // 2
    core = place_ref[0] % 2
    for source, at_core in ((pair_ref, core), (other_ref, 1 - core)):
        for step in range(2):
            block = source[step * shard : (step + 1) * shard, :]
            chip = x_lo if step == 0 else 1 - x_lo
            index = chip * 2 + at_core
            weight_ref[pl.ds(pl.multiple_of(index * shard, shard), shard), :] = block
            back = half + (3 - index) * shard
            weight_ref[pl.ds(pl.multiple_of(back, shard), shard), :] = reverse_both(block)
    weight = weight_ref[...]
    values_ref[HALO:, :] = dot(normed_ref[...], weight).astype(BF16).astype(F32)
    values_ref[0:HALO, :] = dot(tail_ref[...], weight).astype(BF16).astype(F32)


def mirror_forward_kernel(normed_ref, weight_ref, values_ref):
    values_ref[...] = dot(reverse_both(normed_ref[...]), weight_ref[...]).astype(BF16).astype(F32)


def one_hot(row, count):
    classes = lax.broadcasted_iota(jnp.int32, (HALO, count), 0)
    return (row.astype(jnp.int32) == classes).astype(F32)


def rows_of(hot, table):
    return lax.dot_general(
        hot, table, (((0,), (0,)), ((), ())), preferred_element_type=F32, precision=HIGHEST
    )


def gate_kernel(
    slab_ref, values0_ref, values1_ref, weight_ref, grad_ref, head_ref, tokens_ref,
    filter_ref, filter_rev_ref, bias_ref, bias_rev_ref,
    value_grad_ref, send_ref, terms_ref,
    wide0, wide1, pull0, pull1,
):
    rows = grad_ref.shape[0]
    taps = filter_ref.shape[0]
    width = grad_ref.shape[1]
    reach = rows + HALO
    token_row = slab_ref[reach:, :].astype(F32)[HALO - 1 : HALO, :]
    hot1_own = one_hot(token_row[:, :LANES], LANES)
    hot1_far = one_hot(token_row[:, LANES : 2 * LANES], LANES)
    hot0_own = one_hot(tokens_ref[...], LANES)
    hot0_far = one_hot(head_ref[...].astype(F32)[HALO - 1 : HALO, :LANES], LANES)
    edge = dot(slab_ref[reach:, :], weight_ref[...]).astype(BF16).astype(F32)
    values1_edge = edge
    wide = 2 * LANES

    for index in range(width // wide):
        cols = slice(index * wide, (index + 1) * wide)
        taps0 = filter_ref[:, cols]
        taps1 = filter_rev_ref[:, cols]
        wide0[...] = values0_ref[:, cols]
        wide1[0:rows, :] = values1_ref[:, cols]
        wide1[rows:, :] = values1_edge[:, cols]
        bias0 = rows_of(hot0_own, bias_ref[:, cols])
        bias0_far = rows_of(hot0_far, bias_ref[:, cols])
        bias1 = rows_of(hot1_own, bias_rev_ref[:, cols])
        bias1_far = rows_of(hot1_far, bias_rev_ref[:, cols])
        own0 = grad_ref[:, cols].astype(F32)
        own1 = slab_ref[HALO:reach, cols].astype(F32)
        gate0 = jax.nn.sigmoid(wide1[0:rows, :] + bias0)
        gate1 = jax.nn.sigmoid(wide0[HALO:, :] + bias1)
        conv_grad0 = own0 * gate0
        conv_grad1 = own1 * gate1
        pull0[0:rows, :] = conv_grad0
        pull1[HALO:, :] = conv_grad1
        pull0[rows:, :] = head_ref[:, cols].astype(F32) * jax.nn.sigmoid(wide1[rows:, :] + bias0_far[0:HALO])
        pull1[0:HALO, :] = slab_ref[0:HALO, cols].astype(F32) * jax.nn.sigmoid(
            wide0[0:HALO, :] + bias1_far[LANES - HALO :]
        )
        conv0 = jnp.zeros((rows, wide), F32)
        conv1 = jnp.zeros((rows, wide), F32)
        for tap in range(taps):
            shifted0 = wide0[HALO - tap : HALO - tap + rows, :]
            shifted1 = wide1[tap : tap + rows, :]
            conv0 = conv0 + taps0[tap : tap + 1] * shifted0
            conv1 = conv1 + taps1[tap : tap + 1] * shifted1
            terms_ref[tap : tap + 1, cols] = jnp.sum(conv_grad0 * shifted0, axis=0, keepdims=True)
            terms_ref[16 + tap : 17 + tap, cols] = jnp.sum(conv_grad1 * shifted1, axis=0, keepdims=True)
        pre0 = own0 * conv0 * gate0 * (1.0 - gate0)
        pre1 = own1 * conv1 * gate1 * (1.0 - gate1)
        terms_ref[8:16, cols] = jnp.dot(hot0_own, pre0, preferred_element_type=F32, precision=HIGHEST)
        terms_ref[24:32, cols] = jnp.dot(hot1_own, pre1, preferred_element_type=F32, precision=HIGHEST)
        total0 = pre1.astype(BF16).astype(F32)
        total1 = pre0.astype(BF16).astype(F32)
        for tap in range(taps):
            total0 = total0 + taps0[tap : tap + 1] * pull0[tap : tap + rows, :]
            total1 = total1 + taps1[tap : tap + 1] * pull1[HALO - tap : HALO - tap + rows, :]
        value_grad_ref[:, cols] = total0.astype(BF16)
        send_ref[0:rows, cols] = total1.astype(BF16)
    unused = jnp.zeros((1, width), F32)
    terms_ref[7:8, :] = unused
    terms_ref[23:24, :] = unused
    send_ref[rows:, :] = terms_ref[16:, :].astype(BF16)


def operands_kernel(normed_ref, value_grad_ref, left_ref, right_ref):
    rows = normed_ref.shape[1]
    half = normed_ref.shape[2] // 2
    for strand in range(2):
        value = normed_ref[strand]
        left_ref[strand * rows : (strand + 1) * rows, :] = value[:, :half]
        left_ref[(2 + strand) * rows : (3 + strand) * rows, :] = reverse_both(value)[:, :half]
    right_ref[0:rows, :] = value_grad_ref[...]
    right_ref[rows:, :] = reverse_both(value_grad_ref[...])


def project_kernel(
    place_ref, scale, left_ref, right_ref, back_ref, terms_ref, value_grad_ref,
    send_ref, keep_ref, sums_ref, final_ref,
):
    rows = right_ref.shape[0] // 2
    back = back_ref[0:rows, :]
    home = reverse_both(back)
    final_ref[0] = right_ref[0:rows, :]
    final_ref[1] = home
    right = jnp.concatenate([right_ref[0:rows, :], home, right_ref[rows:, :], back], axis=0)
    sums = (terms_ref[0:16, :] + reverse_lanes(back_ref[rows:, :]).astype(F32)) * scale
    sums_ref[...] = sums
    core = place_ref[0] % 2
    shard = left_ref.shape[1] // 4
    for chip in range(2):
        for mine in range(2):
            index = chip * 2 + (core if mine else 1 - core)
            left = left_ref[:, pl.ds(pl.multiple_of(index * shard, shard), shard)]
            part = lax.dot_general(left, right, (((0,), (0,)), ((), ())), preferred_element_type=F32) * scale
            if mine:
                keep_ref[chip * shard : (chip + 1) * shard, :] = part
            else:
                send_ref[chip * shard : (chip + 1) * shard, :] = part.astype(BF16)
    send_ref[2 * shard :, :] = sums.astype(BF16)


def input_grad_kernel(value_grad_ref, weight_ref, out_ref):
    weight = weight_ref[...]
    for strand in range(2):
        out_ref[strand] = lax.dot_general(
            value_grad_ref[strand], weight, (((1,), (1,)), ((), ())), preferred_element_type=F32
        ).astype(BF16)


def first_sum_kernel(place_ref, keep_ref, got_ref, sums_ref, send_ref, keep_out_ref, sums_out_ref):
    shard = keep_ref.shape[0] // 2
    x_lo = place_ref[0] // 2
    here = pl.ds(pl.multiple_of(x_lo * shard, shard), shard)
    there = pl.ds(pl.multiple_of((1 - x_lo) * shard, shard), shard)
    keep_out_ref[...] = keep_ref[here, :] + got_ref[here, :].astype(F32)
    send_ref[0:shard, :] = (keep_ref[there, :] + got_ref[there, :].astype(F32)).astype(BF16)
    sums = sums_ref[...] + got_ref[2 * shard :, :].astype(F32)
    sums_out_ref[...] = sums
    send_ref[shard:, :] = sums.astype(BF16)


def last_sum_kernel(place_ref, keep_ref, got_ref, sums_ref, proj_ref, filter_ref, bias_ref):
    shard = keep_ref.shape[0]
    part = filter_ref.shape[1]
    proj_ref[...] = keep_ref[...] + got_ref[0:shard, :].astype(F32)
    cols = pl.ds(pl.multiple_of(place_ref[0] * part, part), part)
    sums = sums_ref[:, cols] + got_ref[shard:, cols].astype(F32)
    filter_ref[...] = sums[0 : filter_ref.shape[0], :]
    bias_ref[...] = sums[8 : 8 + bias_ref.shape[0], :]


def mirrored(value):
    size = lax.axis_size("ctx")
    return lax.ppermute(value, "ctx", [(i, size - 1 - i) for i in range(size)])


def shifted(value, distance):
    devices = range(lax.axis_size("ctx"))
    return lax.ppermute(value, "ctx", [(i, i + distance) for i in devices if i + distance in devices])


def partner(value, bit):
    return lax.ppermute(value, "fsdp", [(i, i ^ bit) for i in range(lax.axis_size("fsdp"))])


def shape(dims, dtype):
    return jax.ShapeDtypeStruct(dims, dtype)


def after(value, *others):
    return lax.optimization_barrier((value, *others))[0]


def shards(normed, out_grad, ids, mask, proj_half, conv_filter, gate_bias):
    rows, width = normed.shape[2], normed.shape[3]
    taps = conv_filter.shape[0]
    shard = proj_half.shape[0]
    classes = gate_bias.shape[0]
    normed = normed[:, 0]
    out_grad = out_grad[:, 0]
    place = lax.axis_index("fsdp").astype(jnp.int32).reshape(1)
    tokens = jnp.where(mask == 1, 5, ids)[:, 0]

    normed_far = mirrored(normed[1])
    tails = shifted(normed[:, rows - HALO :, :], 1)
    token_rows = jnp.pad(tokens.astype(F32).astype(BF16), ((0, 0), (0, width - rows)))
    heads = jnp.concatenate([out_grad[:, : HALO - 1, :], token_rows[:, None, :]], axis=1)
    heads = shifted(heads, -1)
    near = partner(proj_half, 2)

    slab, = call(
        pack_kernel, (shape((rows + 2 * HALO, width), BF16),),
        out_grad[1], tokens[1:2], tails[1], heads[1],
        flops=2 * rows * width * 300, moved=4 * rows * width,
    )
    slab = mirrored(slab)
    pair = jnp.concatenate([proj_half, near], axis=0)
    other = partner(pair, 1)
    filter_rev = conv_filter[:, ::-1]
    bias = jnp.pad(gate_bias, ((0, HALO - classes), (0, 0)))
    bias_rev = bias[:, ::-1]

    weight, values0 = call(
        forward_kernel,
        (shape((width, width), BF16), shape((rows + HALO, width), F32)),
        place, pair, other, normed[0], tails[0], scalars=1,
        flops=2 * rows * width * width, moved=6 * width * width,
    )
    values1, = call(
        mirror_forward_kernel, (shape((rows, width), F32),), normed_far, weight,
        flops=2 * rows * width * width, moved=4 * width * width,
    )
    reach = rows + HALO
    wide = 2 * LANES
    value_grad, send, terms = call(
        gate_kernel,
        (shape((rows, width), BF16), shape((rows + 16, width), BF16), shape((32, width), F32)),
        slab, values0, values1, weight, out_grad[0], heads[0], tokens[0:1],
        conv_filter, filter_rev, bias, bias_rev,
        scratch=[pltpu.VMEM((reach, wide), F32)] * 4,
        flops=2 * rows * width * width, moved=4 * width * width,
    )
    back = mirrored(send)
    left, right = call(
        operands_kernel, (shape((4 * rows, width // 2), BF16), shape((2 * rows, width), BF16)),
        normed, value_grad, flops=rows * width * width, moved=8 * rows * width,
    )
    grad_scale = 1.0 / math.sqrt(2.0 * lax.axis_size("fsdp") * rows)
    send1, keep1, sums1, final = call(
        lambda place_ref, *refs: project_kernel(place_ref, grad_scale, *refs),
        (
            shape((2 * shard + 16, width), BF16),
            shape((2 * shard, width), F32),
            shape((16, width), F32),
            shape((2, rows, width), BF16),
        ),
        place, left, right, back, terms, value_grad, scalars=1,
        flops=4 * rows * width * width, moved=4 * width * width,
    )
    got1 = partner(send1, 1)
    in_grad, = call(
        input_grad_kernel, (shape((2, rows, width), BF16),), final, weight,
        flops=4 * rows * width * width, moved=4 * width * width,
    )
    send2, keep2, sums2 = call(
        first_sum_kernel,
        (shape((shard + 16, width), BF16), shape((shard, width), F32), shape((16, width), F32)),
        place, keep1, got1, sums1, scalars=1, moved=16 * shard * width,
    )
    got2 = partner(send2, 2)
    part = width // lax.axis_size("fsdp")
    proj_grad, filter_grad, bias_grad = call(
        last_sum_kernel,
        (shape((shard, width), F32), shape((taps, part), F32), shape((classes, part), F32)),
        place, keep2, got2, sums2, scalars=1, moved=12 * shard * width,
    )
    return in_grad[:, None], proj_grad[None], filter_grad[None], bias_grad[None]


def solution(mesh):
    placed = (
        P(None, "fsdp", "ctx", None),
        P(None, "fsdp", "ctx", None),
        P(None, "fsdp", "ctx"),
        P(None, "fsdp", "ctx"),
        P("fsdp", None),
        P(),
        P(),
    )
    return jax.shard_map(
        shards,
        mesh=mesh,
        in_specs=placed,
        out_specs=(
            P(None, "fsdp", "ctx", None),
            P("ctx", "fsdp", None),
            P("ctx", None, "fsdp"),
            P("ctx", None, "fsdp"),
        ),
        check_vma=False,
    )
```

```python
import math

import jax
import jax.numpy as jnp
from jax import lax
from jax.experimental import pallas as pl
from jax.experimental.pallas import tpu as pltpu
from jax.sharding import PartitionSpec as P


LANES = 128
HALO = 8
F32 = jnp.float32
BF16 = jnp.bfloat16
HIGHEST = lax.Precision.HIGHEST


def dot(a, b):
    return jnp.dot(a, b, preferred_element_type=F32)


def reversal(size, dtype=BF16):
    rows = lax.broadcasted_iota(jnp.int32, (size, size), 0)
    cols = lax.broadcasted_iota(jnp.int32, (size, size), 1)
    return (rows + cols == size - 1).astype(dtype)


def reverse_lanes(value, precision=None):
    count = value.shape[-1] // LANES
    swap = reversal(LANES, value.dtype)
    parts = []
    for block in reversed(range(count)):
        part = value[:, block * LANES : (block + 1) * LANES]
        parts.append(
            jnp.dot(part, swap, preferred_element_type=F32, precision=precision).astype(value.dtype)
        )
    return jnp.concatenate(parts, axis=1)


def reverse_rows(value):
    return dot(reversal(value.shape[0]), value).astype(value.dtype)


def reverse_both(value):
    return reverse_lanes(reverse_rows(value))


def call(kernel, out_shapes, *operands, scalars=0, scratch=(), flops=0, moved=0):
    specs = [pl.BlockSpec(memory_space=pltpu.SMEM)] * scalars
    specs += [pl.BlockSpec(memory_space=pltpu.VMEM)] * (len(operands) - scalars)
    return pl.pallas_call(
        kernel,
        out_shape=out_shapes,
        in_specs=specs,
        out_specs=[pl.BlockSpec(memory_space=pltpu.VMEM)] * len(out_shapes),
        scratch_shapes=list(scratch),
        cost_estimate=pl.CostEstimate(flops=flops, bytes_accessed=moved, transcendentals=0),
        compiler_params=pltpu.CompilerParams(vmem_limit_bytes=48 * 1024 * 1024),
    )(*operands)


def token_row(ids_ref, mask_ref, strand):
    return jnp.where(mask_ref[strand] == 1, 5, ids_ref[strand]).astype(F32)


def halo_kernel(normed_ref, grad_ref, ids_ref, mask_ref, tails_ref, heads_ref):
    rows = normed_ref.shape[1]
    tails_ref[...] = normed_ref[:, rows - HALO :, :]
    width = grad_ref.shape[2]
    at_row = lax.broadcasted_iota(jnp.int32, (HALO, width), 0) == HALO - 1
    for strand in range(2):
        tokens = token_row(ids_ref, mask_ref, strand)
        tokens = jnp.concatenate([tokens, jnp.zeros((1, width - LANES), F32)], axis=1)
        heads_ref[strand] = jnp.where(at_row, tokens, grad_ref[strand, 0:HALO, :].astype(F32)).astype(BF16)


def pack_kernel(grad_ref, ids_ref, mask_ref, tails_ref, heads_ref, slab_ref):
    rows, width = grad_ref.shape[1], grad_ref.shape[2]
    head = heads_ref[1].astype(F32)
    swap = reversal(HALO, F32)
    tail_rev = jnp.dot(swap, tails_ref[1].astype(F32), preferred_element_type=F32).astype(BF16)
    head_rev = jnp.dot(swap, head, preferred_element_type=F32).astype(BF16)
    own = token_row(ids_ref, mask_ref, 1)
    both = jnp.concatenate([own, head[HALO - 1 : HALO, :LANES], jnp.zeros((6, LANES), F32)], axis=0)
    flipped = dot(both.astype(BF16), reversal(LANES))
    tokens = jnp.concatenate([flipped[0:1], flipped[1:2], jnp.zeros((1, width - 2 * LANES), F32)], axis=1)
    at_row = lax.broadcasted_iota(jnp.int32, (HALO, width), 0) == HALO - 1
    slab_ref[0:HALO, :] = reverse_lanes(head_rev)
    slab_ref[HALO : HALO + rows, :] = reverse_both(grad_ref[1])
    slab_ref[HALO + rows :, :] = jnp.where(at_row, tokens, reverse_lanes(tail_rev).astype(F32)).astype(BF16)


def forward_kernel(place_ref, own_ref, near_ref, other_ref, normed_ref, tails_ref, weight_ref, values_ref):
    shard = own_ref.shape[0]
    half = 4 * shard
    x_lo = place_ref[0] // 2
    core = place_ref[0] % 2
    pieces = (
        (own_ref[...], x_lo, core),
        (near_ref[...], 1 - x_lo, core),
        (other_ref[0:shard, :], x_lo, 1 - core),
        (other_ref[shard:, :], 1 - x_lo, 1 - core),
    )
    for block, chip, at_core in pieces:
        index = chip * 2 + at_core
        weight_ref[pl.ds(pl.multiple_of(index * shard, shard), shard), :] = block
        back = half + (3 - index) * shard
        weight_ref[pl.ds(pl.multiple_of(back, shard), shard), :] = reverse_both(block)
    weight = weight_ref[...]
    values_ref[HALO:, :] = dot(normed_ref[0], weight).astype(BF16).astype(F32)
    values_ref[0:HALO, :] = dot(tails_ref[0], weight).astype(BF16).astype(F32)


def one_hot(row, count):
    classes = lax.broadcasted_iota(jnp.int32, (HALO, count), 0)
    return (row.astype(jnp.int32) == classes).astype(F32)


def rows_of(hot, table):
    return lax.dot_general(
        hot, table, (((0,), (0,)), ((), ())), preferred_element_type=F32, precision=HIGHEST
    )


def near_strand_kernel(
    far_ref, weight_ref, values0_ref, grad_ref, ids_ref, mask_ref, filter_ref, bias_ref,
    values1_ref, conv_grad_ref, mirror_ref, terms_ref,
):
    rows, width = grad_ref.shape[1], grad_ref.shape[2]
    taps = filter_ref.shape[0]
    values1_ref[...] = dot(reverse_both(far_ref[...]), weight_ref[...]).astype(BF16).astype(F32)
    hot = one_hot(token_row(ids_ref, mask_ref, 0), LANES)
    wide = 2 * LANES
    for index in range(width // wide):
        cols = slice(index * wide, (index + 1) * wide)
        weights = filter_ref[:, cols]
        own = grad_ref[0, :, cols].astype(F32)
        gate = jax.nn.sigmoid(values1_ref[:, cols] + rows_of(hot, bias_ref[:, cols]))
        conv_grad = own * gate
        conv_grad_ref[:, cols] = conv_grad
        conv = jnp.zeros((rows, wide), F32)
        for tap in range(taps):
            shifted = values0_ref[HALO - tap : HALO - tap + rows, cols]
            conv = conv + weights[tap : tap + 1] * shifted
            terms_ref[tap : tap + 1, cols] = jnp.sum(conv_grad * shifted, axis=0, keepdims=True)
        pre = own * conv * gate * (1.0 - gate)
        mirror_ref[:, cols] = pre.astype(BF16)
        terms_ref[8:16, cols] = jnp.dot(hot, pre, preferred_element_type=F32, precision=HIGHEST)
    terms_ref[7:8, :] = jnp.zeros((1, width), F32)


def far_strand_kernel(
    slab_ref, weight_ref, values0_ref, values1_ref, mirror_ref, heads_ref,
    filter_rev_ref, bias_ref, bias_rev_ref,
    send_ref, mirror_out_ref, edge_ref,
    wide1, pull1, sums,
):
    rows, width = mirror_ref.shape
    taps = filter_rev_ref.shape[0]
    reach = rows + HALO
    tokens = slab_ref[reach:, :].astype(F32)[HALO - 1 : HALO, :]
    hot_own = one_hot(tokens[:, :LANES], LANES)
    hot_far = one_hot(tokens[:, LANES : 2 * LANES], LANES)
    hot_edge = one_hot(heads_ref[0].astype(F32)[HALO - 1 : HALO, :LANES], LANES)
    edge = dot(slab_ref[reach:, :], weight_ref[...]).astype(BF16).astype(F32)
    edge_gate = jax.nn.sigmoid(edge + rows_of(hot_edge, bias_ref[...])[0:HALO])
    edge_ref[...] = heads_ref[0].astype(F32) * edge_gate
    sums[...] = jnp.zeros_like(sums)
    wide = 2 * LANES
    for index in range(width // wide):
        cols = slice(index * wide, (index + 1) * wide)
        weights = filter_rev_ref[:, cols]
        wide1[0:rows, :] = values1_ref[:, cols]
        wide1[rows:, :] = edge[:, cols]
        own = slab_ref[HALO:reach, cols].astype(F32)
        gate = jax.nn.sigmoid(values0_ref[HALO:, cols] + rows_of(hot_own, bias_rev_ref[:, cols]))
        far_gate = jax.nn.sigmoid(
            values0_ref[0:HALO, cols] + rows_of(hot_far, bias_rev_ref[:, cols])[LANES - HALO :]
        )
        conv_grad = own * gate
        pull1[HALO:, :] = conv_grad
        pull1[0:HALO, :] = slab_ref[0:HALO, cols].astype(F32) * far_gate
        conv = jnp.zeros((rows, wide), F32)
        for tap in range(taps):
            shifted = wide1[tap : tap + rows, :]
            conv = conv + weights[tap : tap + 1] * shifted
            sums[tap : tap + 1, cols] = jnp.sum(conv_grad * shifted, axis=0, keepdims=True)
        pre = own * conv * gate * (1.0 - gate)
        mirror_out_ref[:, cols] = pre.astype(BF16)
        sums[8:16, cols] = jnp.dot(hot_own, pre, preferred_element_type=F32, precision=HIGHEST)
        total = mirror_ref[:, cols].astype(F32)
        for tap in range(taps):
            total = total + weights[tap : tap + 1] * pull1[HALO - tap : HALO - tap + rows, :]
        send_ref[0:rows, cols] = total.astype(BF16)
    send_ref[rows:, :] = sums[...].astype(BF16)


def operands_kernel(
    normed_ref, conv_grad_ref, edge_ref, mirror_ref, filter_ref, left_ref, right_ref, pull0,
):
    rows, width = conv_grad_ref.shape
    half = width // 2
    pull0[0:rows, :] = conv_grad_ref[...]
    pull0[rows:, :] = edge_ref[...]
    for strand in range(2):
        value = normed_ref[strand]
        left_ref[strand * rows : (strand + 1) * rows, :] = value[:, :half]
        left_ref[(2 + strand) * rows : (3 + strand) * rows, :] = reverse_both(value)[:, :half]
    wide = 2 * LANES
    for index in range(width // wide):
        cols = slice(index * wide, (index + 1) * wide)
        total = mirror_ref[:, cols].astype(F32)
        for tap in range(filter_ref.shape[0]):
            total = total + filter_ref[tap : tap + 1, cols] * pull0[tap : tap + rows, cols]
        right_ref[0:rows, cols] = total.astype(BF16)
    right_ref[rows:, :] = reverse_both(right_ref[0:rows, :])


def project_kernel(
    place_ref, scale, left_ref, right_ref, back_ref, terms_ref,
    send_ref, keep_ref, sums_ref, final_ref,
):
    rows = right_ref.shape[0] // 2
    back = back_ref[0:rows, :]
    home = reverse_both(back)
    final_ref[0] = right_ref[0:rows, :]
    final_ref[1] = home
    right = jnp.concatenate([right_ref[0:rows, :], home, right_ref[rows:, :], back], axis=0)
    sums = (terms_ref[...] + reverse_lanes(back_ref[rows:, :]).astype(F32)) * scale
    sums_ref[...] = sums
    core = place_ref[0] % 2
    shard = left_ref.shape[1] // 4
    for chip in range(2):
        for mine in range(2):
            index = chip * 2 + (core if mine else 1 - core)
            left = left_ref[:, pl.ds(pl.multiple_of(index * shard, shard), shard)]
            part = lax.dot_general(left, right, (((0,), (0,)), ((), ())), preferred_element_type=F32) * scale
            if mine:
                keep_ref[chip * shard : (chip + 1) * shard, :] = part
            else:
                send_ref[chip * shard : (chip + 1) * shard, :] = part.astype(BF16)
    send_ref[2 * shard :, :] = sums.astype(BF16)


def input_grad_kernel(value_grad_ref, weight_ref, out_ref):
    weight = weight_ref[...]
    for strand in range(2):
        out_ref[strand] = lax.dot_general(
            value_grad_ref[strand], weight, (((1,), (1,)), ((), ())), preferred_element_type=F32
        ).astype(BF16)


def first_sum_kernel(place_ref, keep_ref, got_ref, sums_ref, send_ref, keep_out_ref, sums_out_ref):
    shard = keep_ref.shape[0] // 2
    x_lo = place_ref[0] // 2
    here = pl.ds(pl.multiple_of(x_lo * shard, shard), shard)
    there = pl.ds(pl.multiple_of((1 - x_lo) * shard, shard), shard)
    keep_out_ref[...] = keep_ref[here, :] + got_ref[here, :].astype(F32)
    send_ref[0:shard, :] = (keep_ref[there, :] + got_ref[there, :].astype(F32)).astype(BF16)
    sums = sums_ref[...] + got_ref[2 * shard :, :].astype(F32)
    sums_out_ref[...] = sums
    send_ref[shard:, :] = sums.astype(BF16)


def last_sum_kernel(place_ref, keep_ref, got_ref, sums_ref, proj_ref, filter_ref, bias_ref):
    shard = keep_ref.shape[0]
    part = filter_ref.shape[2]
    proj_ref[...] = keep_ref[...] + got_ref[0:shard, :].astype(F32)
    cols = pl.ds(pl.multiple_of(place_ref[0] * part, part), part)
    sums = sums_ref[:, cols] + got_ref[shard:, cols].astype(F32)
    for tap in range(filter_ref.shape[0]):
        filter_ref[tap] = sums[tap : tap + 1, :]
    for token in range(bias_ref.shape[0]):
        bias_ref[token] = sums[8 + token : 9 + token, :]


def mirrored(value):
    size = lax.axis_size("ctx")
    return lax.ppermute(value, "ctx", [(i, size - 1 - i) for i in range(size)])


def shifted(value, distance):
    devices = range(lax.axis_size("ctx"))
    return lax.ppermute(value, "ctx", [(i, i + distance) for i in devices if i + distance in devices])


def partner(value, bit):
    return lax.ppermute(value, "fsdp", [(i, i ^ bit) for i in range(lax.axis_size("fsdp"))])


def shape(dims, dtype):
    return jax.ShapeDtypeStruct(dims, dtype)


def step(normed, out_grad, ids, mask, proj_half, conv_filter, gate_bias):
    rows, width = normed.shape[2], normed.shape[3]
    taps = conv_filter.shape[0]
    shard = proj_half.shape[0]
    classes = gate_bias.shape[0]
    normed, out_grad = normed[:, 0], out_grad[:, 0]
    place = lax.axis_index("fsdp").astype(jnp.int32).reshape(1)

    normed_far = mirrored(normed[1])
    tails, heads = call(
        halo_kernel, (shape((2, HALO, width), BF16), shape((2, HALO, width), BF16)),
        normed, out_grad, ids, mask,
        moved=16 * HALO * width,
    )
    heads = shifted(heads, -1)
    tails = shifted(tails, 1)
    near = partner(proj_half, 2)
    slab, = call(
        pack_kernel, (shape((rows + 2 * HALO, width), BF16),),
        out_grad, ids, mask, tails, heads,
        flops=600 * rows * width, moved=4 * rows * width,
    )
    slab = mirrored(slab)
    other = partner(jnp.concatenate([proj_half, near], axis=0), 1)
    filter_rev = conv_filter[:, ::-1]
    bias = jnp.pad(gate_bias, ((0, HALO - classes), (0, 0)))
    bias_rev = bias[:, ::-1]

    weight, values0 = call(
        forward_kernel,
        (shape((width, width), BF16), shape((rows + HALO, width), F32)),
        place, proj_half, near, other, normed, tails, scalars=1,
        flops=2 * rows * width * width, moved=6 * width * width,
    )
    values1, conv_grad, mirror0, terms = call(
        near_strand_kernel,
        (
            shape((rows, width), F32),
            shape((rows, width), F32),
            shape((rows, width), BF16),
            shape((16, width), F32),
        ),
        normed_far, weight, values0, out_grad, ids, mask, conv_filter, bias,
        flops=2 * rows * width * width, moved=8 * width * width,
    )
    wide = 2 * LANES
    send, mirror1, edge = call(
        far_strand_kernel,
        (shape((rows + 16, width), BF16), shape((rows, width), BF16), shape((HALO, width), F32)),
        slab, weight, values0, values1, mirror0, heads, filter_rev, bias, bias_rev,
        scratch=[pltpu.VMEM((rows + HALO, wide), F32)] * 2 + [pltpu.VMEM((16, width), F32)],
        flops=2 * rows * width * width, moved=8 * width * width,
    )
    back = mirrored(send)
    left, right = call(
        operands_kernel, (shape((4 * rows, width // 2), BF16), shape((2 * rows, width), BF16)),
        normed, conv_grad, edge, mirror1, conv_filter,
        scratch=[pltpu.VMEM((rows + HALO, width), F32)],
        flops=rows * width * width, moved=16 * rows * width,
    )
    grad_scale = 1.0 / math.sqrt(2.0 * lax.axis_size("fsdp") * rows)
    send1, keep1, sums1, final = call(
        lambda place_ref, *refs: project_kernel(place_ref, grad_scale, *refs),
        (
            shape((2 * shard + 16, width), BF16),
            shape((2 * shard, width), F32),
            shape((16, width), F32),
            shape((2, rows, width), BF16),
        ),
        place, left, right, back, terms, scalars=1,
        flops=4 * rows * width * width, moved=4 * width * width,
    )
    got1 = partner(send1, 1)
    send2, keep2, sums2 = call(
        first_sum_kernel,
        (shape((shard + 16, width), BF16), shape((shard, width), F32), shape((16, width), F32)),
        place, keep1, got1, sums1, scalars=1, moved=16 * shard * width,
    )
    got2 = partner(send2, 2)
    in_grad, = call(
        input_grad_kernel, (shape((2, rows, width), BF16),), final, weight,
        flops=4 * rows * width * width, moved=4 * width * width,
    )
    part = width // lax.axis_size("fsdp")
    proj_grad, filter_grad, bias_grad = call(
        last_sum_kernel,
        (shape((shard, width), F32), shape((taps, 1, part), F32), shape((classes, 1, part), F32)),
        place, keep2, got2, sums2, scalars=1, moved=12 * shard * width,
    )
    return (
        in_grad[:, None],
        proj_grad[None],
        jnp.transpose(filter_grad, (1, 0, 2)),
        jnp.transpose(bias_grad, (1, 0, 2)),
    )


def solution(mesh):
    placed = (
        P(None, "fsdp", "ctx", None),
        P(None, "fsdp", "ctx", None),
        P(None, "fsdp", "ctx"),
        P(None, "fsdp", "ctx"),
        P("fsdp", None),
        P(),
        P(),
    )
    return jax.shard_map(
        step,
        mesh=mesh,
        in_specs=placed,
        out_specs=(
            P(None, "fsdp", "ctx", None),
            P("ctx", "fsdp", None),
            P("ctx", None, "fsdp"),
            P("ctx", None, "fsdp"),
        ),
        check_vma=False,
    )
```

```python
import math

import jax
import jax.numpy as jnp
from jax import lax
from jax.experimental import pallas as pl
from jax.experimental.pallas import tpu as pltpu
from jax.sharding import PartitionSpec as P


LANES = 128
HALO = 8
F32 = jnp.float32
BF16 = jnp.bfloat16
HIGHEST = lax.Precision.HIGHEST


def dot(a, b):
    return jnp.dot(a, b, preferred_element_type=F32)


def reversal(size, dtype=BF16):
    rows = lax.broadcasted_iota(jnp.int32, (size, size), 0)
    cols = lax.broadcasted_iota(jnp.int32, (size, size), 1)
    return (rows + cols == size - 1).astype(dtype)


def reverse_lanes(value, precision=None):
    count = value.shape[-1] // LANES
    swap = reversal(LANES, value.dtype)
    parts = []
    for block in reversed(range(count)):
        part = value[:, block * LANES : (block + 1) * LANES]
        parts.append(
            jnp.dot(part, swap, preferred_element_type=F32, precision=precision).astype(value.dtype)
        )
    return jnp.concatenate(parts, axis=1)


def reverse_rows(value):
    return dot(reversal(value.shape[0]), value).astype(value.dtype)


def reverse_both(value):
    return reverse_lanes(reverse_rows(value))


def call(kernel, out_shapes, *operands, scalars=0, scratch=(), flops=0, moved=0):
    specs = [pl.BlockSpec(memory_space=pltpu.SMEM)] * scalars
    specs += [pl.BlockSpec(memory_space=pltpu.VMEM)] * (len(operands) - scalars)
    return pl.pallas_call(
        kernel,
        out_shape=out_shapes,
        in_specs=specs,
        out_specs=[pl.BlockSpec(memory_space=pltpu.VMEM)] * len(out_shapes),
        scratch_shapes=list(scratch),
        cost_estimate=pl.CostEstimate(flops=flops, bytes_accessed=moved, transcendentals=0),
        compiler_params=pltpu.CompilerParams(vmem_limit_bytes=48 * 1024 * 1024),
    )(*operands)


def token_row(ids_ref, mask_ref, strand):
    return jnp.where(mask_ref[strand] == 1, 5, ids_ref[strand]).astype(F32)


def halo_kernel(normed_ref, grad_ref, ids_ref, mask_ref, tails_ref, heads_ref):
    rows = normed_ref.shape[1]
    tails_ref[...] = normed_ref[:, rows - HALO :, :]
    width = grad_ref.shape[2]
    at_row = lax.broadcasted_iota(jnp.int32, (HALO, width), 0) == HALO - 1
    for strand in range(2):
        tokens = token_row(ids_ref, mask_ref, strand)
        tokens = jnp.concatenate([tokens, jnp.zeros((1, width - LANES), F32)], axis=1)
        heads_ref[strand] = jnp.where(at_row, tokens, grad_ref[strand, 0:HALO, :].astype(F32)).astype(BF16)


def flip_kernel(grad_ref, out_ref, block, arrived):
    copy = pltpu.make_async_copy(grad_ref.at[1], block, arrived)
    copy.start()
    copy.wait()
    out_ref[...] = reverse_both(block[...])


def edge_kernel(ids_ref, mask_ref, tails_ref, heads_ref, slab_ref):
    width = slab_ref.shape[1]
    head = heads_ref[1].astype(F32)
    swap = reversal(HALO, F32)
    tail_rev = jnp.dot(swap, tails_ref[1].astype(F32), preferred_element_type=F32).astype(BF16)
    head_rev = jnp.dot(swap, head, preferred_element_type=F32).astype(BF16)
    own = token_row(ids_ref, mask_ref, 1)
    both = jnp.concatenate([own, head[HALO - 1 : HALO, :LANES], jnp.zeros((6, LANES), F32)], axis=0)
    flipped = dot(both.astype(BF16), reversal(LANES))
    tokens = jnp.concatenate([flipped[0:1], flipped[1:2], jnp.zeros((1, width - 2 * LANES), F32)], axis=1)
    at_row = lax.broadcasted_iota(jnp.int32, (HALO, width), 0) == HALO - 1
    slab_ref[0:HALO, :] = reverse_lanes(head_rev)
    slab_ref[HALO:, :] = jnp.where(at_row, tokens, reverse_lanes(tail_rev).astype(F32)).astype(BF16)


def forward_kernel(place_ref, own_ref, near_ref, other_ref, normed_ref, tails_ref, weight_ref, values_ref):
    shard = own_ref.shape[0]
    half = 4 * shard
    x_lo = place_ref[0] // 2
    core = place_ref[0] % 2
    pieces = (
        (own_ref[...], x_lo, core),
        (near_ref[...], 1 - x_lo, core),
        (other_ref[0:shard, :], x_lo, 1 - core),
        (other_ref[shard:, :], 1 - x_lo, 1 - core),
    )
    for block, chip, at_core in pieces:
        index = chip * 2 + at_core
        weight_ref[pl.ds(pl.multiple_of(index * shard, shard), shard), :] = block
        back = half + (3 - index) * shard
        weight_ref[pl.ds(pl.multiple_of(back, shard), shard), :] = reverse_both(block)
    weight = weight_ref[...]
    values_ref[HALO:, :] = dot(normed_ref[0], weight).astype(BF16).astype(F32)
    values_ref[0:HALO, :] = dot(tails_ref[0], weight).astype(BF16).astype(F32)


def one_hot(row, count):
    classes = lax.broadcasted_iota(jnp.int32, (HALO, count), 0)
    return (row.astype(jnp.int32) == classes).astype(F32)


def rows_of(hot, table):
    return lax.dot_general(
        hot, table, (((0,), (0,)), ((), ())), preferred_element_type=F32, precision=HIGHEST
    )


def near_strand_kernel(
    far_ref, weight_ref, values0_ref, grad_ref, ids_ref, mask_ref, filter_ref, bias_ref,
    values1_ref, conv_grad_ref, mirror_ref, terms_ref,
):
    rows, width = grad_ref.shape[1], grad_ref.shape[2]
    taps = filter_ref.shape[0]
    values1_ref[...] = dot(reverse_both(far_ref[...]), weight_ref[...]).astype(BF16).astype(F32)
    hot = one_hot(token_row(ids_ref, mask_ref, 0), LANES)
    wide = 2 * LANES
    for index in range(width // wide):
        cols = slice(index * wide, (index + 1) * wide)
        weights = filter_ref[:, cols]
        own = grad_ref[0, :, cols].astype(F32)
        gate = jax.nn.sigmoid(values1_ref[:, cols] + rows_of(hot, bias_ref[:, cols]))
        conv_grad = own * gate
        conv_grad_ref[:, cols] = conv_grad
        conv = jnp.zeros((rows, wide), F32)
        for tap in range(taps):
            shifted = values0_ref[HALO - tap : HALO - tap + rows, cols]
            conv = conv + weights[tap : tap + 1] * shifted
            terms_ref[tap : tap + 1, cols] = jnp.sum(conv_grad * shifted, axis=0, keepdims=True)
        pre = own * conv * gate * (1.0 - gate)
        mirror_ref[:, cols] = pre.astype(BF16)
        terms_ref[8:16, cols] = jnp.dot(hot, pre, preferred_element_type=F32, precision=HIGHEST)
    terms_ref[7:8, :] = jnp.zeros((1, width), F32)


def far_strand_kernel(
    slab_ref, halo_ref, weight_ref, values0_ref, values1_ref, mirror_ref, heads_ref,
    filter_rev_ref, bias_ref, bias_rev_ref,
    send_ref, mirror_out_ref, edge_ref,
    wide1, pull1, sums,
):
    rows, width = mirror_ref.shape
    taps = filter_rev_ref.shape[0]
    tokens = halo_ref[HALO:, :].astype(F32)[HALO - 1 : HALO, :]
    hot_own = one_hot(tokens[:, :LANES], LANES)
    hot_far = one_hot(tokens[:, LANES : 2 * LANES], LANES)
    hot_edge = one_hot(heads_ref[0].astype(F32)[HALO - 1 : HALO, :LANES], LANES)
    edge = dot(halo_ref[HALO:, :], weight_ref[...]).astype(BF16).astype(F32)
    edge_gate = jax.nn.sigmoid(edge + rows_of(hot_edge, bias_ref[...])[0:HALO])
    edge_ref[...] = heads_ref[0].astype(F32) * edge_gate
    sums[...] = jnp.zeros_like(sums)
    wide = 2 * LANES
    for index in range(width // wide):
        cols = slice(index * wide, (index + 1) * wide)
        weights = filter_rev_ref[:, cols]
        wide1[0:rows, :] = values1_ref[:, cols]
        wide1[rows:, :] = edge[:, cols]
        own = slab_ref[:, cols].astype(F32)
        gate = jax.nn.sigmoid(values0_ref[HALO:, cols] + rows_of(hot_own, bias_rev_ref[:, cols]))
        far_gate = jax.nn.sigmoid(
            values0_ref[0:HALO, cols] + rows_of(hot_far, bias_rev_ref[:, cols])[LANES - HALO :]
        )
        conv_grad = own * gate
        pull1[HALO:, :] = conv_grad
        pull1[0:HALO, :] = halo_ref[0:HALO, cols].astype(F32) * far_gate
        conv = jnp.zeros((rows, wide), F32)
        for tap in range(taps):
            shifted = wide1[tap : tap + rows, :]
            conv = conv + weights[tap : tap + 1] * shifted
            sums[tap : tap + 1, cols] = jnp.sum(conv_grad * shifted, axis=0, keepdims=True)
        pre = own * conv * gate * (1.0 - gate)
        mirror_out_ref[:, cols] = pre.astype(BF16)
        sums[8:16, cols] = jnp.dot(hot_own, pre, preferred_element_type=F32, precision=HIGHEST)
        total = mirror_ref[:, cols].astype(F32)
        for tap in range(taps):
            total = total + weights[tap : tap + 1] * pull1[HALO - tap : HALO - tap + rows, :]
        send_ref[0:rows, cols] = total.astype(BF16)
    send_ref[rows:, :] = sums[...].astype(BF16)


def operands_kernel(
    normed_ref, conv_grad_ref, edge_ref, mirror_ref, filter_ref, left_ref, right_ref, pull0,
):
    rows, width = conv_grad_ref.shape
    half = width // 2
    pull0[0:rows, :] = conv_grad_ref[...]
    pull0[rows:, :] = edge_ref[...]
    for strand in range(2):
        value = normed_ref[strand]
        left_ref[strand * rows : (strand + 1) * rows, :] = value[:, :half]
        left_ref[(2 + strand) * rows : (3 + strand) * rows, :] = reverse_both(value)[:, :half]
    wide = 2 * LANES
    for index in range(width // wide):
        cols = slice(index * wide, (index + 1) * wide)
        total = mirror_ref[:, cols].astype(F32)
        for tap in range(filter_ref.shape[0]):
            total = total + filter_ref[tap : tap + 1, cols] * pull0[tap : tap + rows, cols]
        right_ref[0:rows, cols] = total.astype(BF16)
    right_ref[rows:, :] = reverse_both(right_ref[0:rows, :])


def project_kernel(
    place_ref, scale, left_ref, right_ref, back_ref, terms_ref,
    send_ref, keep_ref, sums_ref, final_ref,
):
    rows = right_ref.shape[0] // 2
    back = back_ref[0:rows, :]
    home = reverse_both(back)
    final_ref[0] = right_ref[0:rows, :]
    final_ref[1] = home
    right = jnp.concatenate([right_ref[0:rows, :], home, right_ref[rows:, :], back], axis=0)
    sums = (terms_ref[...] + reverse_lanes(back_ref[rows:, :]).astype(F32)) * scale
    sums_ref[...] = sums
    core = place_ref[0] % 2
    shard = left_ref.shape[1] // 4
    for chip in range(2):
        for mine in range(2):
            index = chip * 2 + (core if mine else 1 - core)
            left = left_ref[:, pl.ds(pl.multiple_of(index * shard, shard), shard)]
            part = lax.dot_general(left, right, (((0,), (0,)), ((), ())), preferred_element_type=F32) * scale
            if mine:
                keep_ref[chip * shard : (chip + 1) * shard, :] = part
            else:
                send_ref[chip * shard : (chip + 1) * shard, :] = part.astype(BF16)
    send_ref[2 * shard :, :] = sums.astype(BF16)


def input_grad_kernel(value_grad_ref, weight_ref, out_ref):
    weight = weight_ref[...]
    for strand in range(2):
        out_ref[strand] = lax.dot_general(
            value_grad_ref[strand], weight, (((1,), (1,)), ((), ())), preferred_element_type=F32
        ).astype(BF16)


def first_sum_kernel(place_ref, keep_ref, got_ref, sums_ref, send_ref, keep_out_ref, sums_out_ref):
    shard = keep_ref.shape[0] // 2
    x_lo = place_ref[0] // 2
    here = pl.ds(pl.multiple_of(x_lo * shard, shard), shard)
    there = pl.ds(pl.multiple_of((1 - x_lo) * shard, shard), shard)
    keep_out_ref[...] = keep_ref[here, :] + got_ref[here, :].astype(F32)
    send_ref[0:shard, :] = (keep_ref[there, :] + got_ref[there, :].astype(F32)).astype(BF16)
    sums = sums_ref[...] + got_ref[2 * shard :, :].astype(F32)
    sums_out_ref[...] = sums
    send_ref[shard:, :] = sums.astype(BF16)


def last_sum_kernel(place_ref, keep_ref, got_ref, sums_ref, proj_ref, filter_ref, bias_ref):
    shard = keep_ref.shape[0]
    part = filter_ref.shape[2]
    proj_ref[...] = keep_ref[...] + got_ref[0:shard, :].astype(F32)
    cols = pl.ds(pl.multiple_of(place_ref[0] * part, part), part)
    sums = sums_ref[:, cols] + got_ref[shard:, cols].astype(F32)
    for tap in range(filter_ref.shape[0]):
        filter_ref[tap] = sums[tap : tap + 1, :]
    for token in range(bias_ref.shape[0]):
        bias_ref[token] = sums[8 + token : 9 + token, :]


def mirrored(value):
    size = lax.axis_size("ctx")
    return lax.ppermute(value, "ctx", [(i, size - 1 - i) for i in range(size)])


def shifted(value, distance):
    devices = range(lax.axis_size("ctx"))
    return lax.ppermute(value, "ctx", [(i, i + distance) for i in devices if i + distance in devices])


def partner(value, bit):
    return lax.ppermute(value, "fsdp", [(i, i ^ bit) for i in range(lax.axis_size("fsdp"))])


def shape(dims, dtype):
    return jax.ShapeDtypeStruct(dims, dtype)


def flipped_strand(out_grad):
    rows, width = out_grad.shape[1:]
    return pl.pallas_call(
        flip_kernel,
        out_shape=shape((rows, width), BF16),
        in_specs=[pl.BlockSpec(memory_space=pl.ANY)],
        out_specs=pl.BlockSpec(memory_space=pltpu.VMEM),
        scratch_shapes=[pltpu.VMEM((rows, width), BF16), pltpu.SemaphoreType.DMA],
        cost_estimate=pl.CostEstimate(flops=600 * rows * width, bytes_accessed=4 * rows * width, transcendentals=0),
        compiler_params=pltpu.CompilerParams(vmem_limit_bytes=48 * 1024 * 1024),
    )(out_grad)


def step(normed, out_grad, ids, mask, proj_half, conv_filter, gate_bias):
    rows, width = normed.shape[2], normed.shape[3]
    taps = conv_filter.shape[0]
    shard = proj_half.shape[0]
    classes = gate_bias.shape[0]
    normed, out_grad = normed[:, 0], out_grad[:, 0]
    place = lax.axis_index("fsdp").astype(jnp.int32).reshape(1)

    normed_far = mirrored(normed[1])
    slab = mirrored(flipped_strand(out_grad))
    tails, heads = call(
        halo_kernel, (shape((2, HALO, width), BF16), shape((2, HALO, width), BF16)),
        normed, out_grad, ids, mask,
        moved=16 * HALO * width,
    )
    heads = shifted(heads, -1)
    tails = shifted(tails, 1)
    near = partner(proj_half, 2)
    halo, = call(
        edge_kernel, (shape((2 * HALO, width), BF16),), ids, mask, tails, heads,
        flops=600 * HALO * width, moved=8 * HALO * width,
    )
    halo = mirrored(halo)
    other = partner(jnp.concatenate([proj_half, near], axis=0), 1)
    filter_rev = conv_filter[:, ::-1]
    bias = jnp.pad(gate_bias, ((0, HALO - classes), (0, 0)))
    bias_rev = bias[:, ::-1]

    weight, values0 = call(
        forward_kernel,
        (shape((width, width), BF16), shape((rows + HALO, width), F32)),
        place, proj_half, near, other, normed, tails, scalars=1,
        flops=2 * rows * width * width, moved=6 * width * width,
    )
    values1, conv_grad, mirror0, terms = call(
        near_strand_kernel,
        (
            shape((rows, width), F32),
            shape((rows, width), F32),
            shape((rows, width), BF16),
            shape((16, width), F32),
        ),
        normed_far, weight, values0, out_grad, ids, mask, conv_filter, bias,
        flops=2 * rows * width * width, moved=8 * width * width,
    )
    wide = 2 * LANES
    send, mirror1, edge = call(
        far_strand_kernel,
        (shape((rows + 16, width), BF16), shape((rows, width), BF16), shape((HALO, width), F32)),
        slab, halo, weight, values0, values1, mirror0, heads, filter_rev, bias, bias_rev,
        scratch=[pltpu.VMEM((rows + HALO, wide), F32)] * 2 + [pltpu.VMEM((16, width), F32)],
        flops=2 * rows * width * width, moved=8 * width * width,
    )
    back = mirrored(send)
    left, right = call(
        operands_kernel, (shape((4 * rows, width // 2), BF16), shape((2 * rows, width), BF16)),
        normed, conv_grad, edge, mirror1, conv_filter,
        scratch=[pltpu.VMEM((rows + HALO, width), F32)],
        flops=rows * width * width, moved=16 * rows * width,
    )
    grad_scale = 1.0 / math.sqrt(2.0 * lax.axis_size("fsdp") * rows)
    send1, keep1, sums1, final = call(
        lambda place_ref, *refs: project_kernel(place_ref, grad_scale, *refs),
        (
            shape((2 * shard + 16, width), BF16),
            shape((2 * shard, width), F32),
            shape((16, width), F32),
            shape((2, rows, width), BF16),
        ),
        place, left, right, back, terms, scalars=1,
        flops=4 * rows * width * width, moved=4 * width * width,
    )
    got1 = partner(send1, 1)
    send2, keep2, sums2 = call(
        first_sum_kernel,
        (shape((shard + 16, width), BF16), shape((shard, width), F32), shape((16, width), F32)),
        place, keep1, got1, sums1, scalars=1, moved=16 * shard * width,
    )
    got2 = partner(send2, 2)
    in_grad, = call(
        input_grad_kernel, (shape((2, rows, width), BF16),), final, weight,
        flops=4 * rows * width * width, moved=4 * width * width,
    )
    part = width // lax.axis_size("fsdp")
    proj_grad, filter_grad, bias_grad = call(
        last_sum_kernel,
        (shape((shard, width), F32), shape((taps, 1, part), F32), shape((classes, 1, part), F32)),
        place, keep2, got2, sums2, scalars=1, moved=12 * shard * width,
    )
    return (
        in_grad[:, None],
        proj_grad[None],
        jnp.transpose(filter_grad, (1, 0, 2)),
        jnp.transpose(bias_grad, (1, 0, 2)),
    )


def solution(mesh):
    placed = (
        P(None, "fsdp", "ctx", None),
        P(None, "fsdp", "ctx", None),
        P(None, "fsdp", "ctx"),
        P(None, "fsdp", "ctx"),
        P("fsdp", None),
        P(),
        P(),
    )
    return jax.shard_map(
        step,
        mesh=mesh,
        in_specs=placed,
        out_specs=(
            P(None, "fsdp", "ctx", None),
            P("ctx", "fsdp", None),
            P("ctx", None, "fsdp"),
            P("ctx", None, "fsdp"),
        ),
        check_vma=False,
    )
```

```python
import math

import jax
import jax.numpy as jnp
from jax import lax
from jax.experimental import pallas as pl
from jax.experimental.pallas import tpu as pltpu
from jax.sharding import PartitionSpec as P


LANES = 128
HALO = 8
F32 = jnp.float32
BF16 = jnp.bfloat16
HIGHEST = lax.Precision.HIGHEST


def dot(a, b):
    return jnp.dot(a, b, preferred_element_type=F32)


def reversal(size, dtype=BF16):
    rows = lax.broadcasted_iota(jnp.int32, (size, size), 0)
    cols = lax.broadcasted_iota(jnp.int32, (size, size), 1)
    return (rows + cols == size - 1).astype(dtype)


def reverse_lanes(value, precision=None):
    count = value.shape[-1] // LANES
    swap = reversal(LANES, value.dtype)
    parts = []
    for block in reversed(range(count)):
        part = value[:, block * LANES : (block + 1) * LANES]
        parts.append(
            jnp.dot(part, swap, preferred_element_type=F32, precision=precision).astype(value.dtype)
        )
    return jnp.concatenate(parts, axis=1)


def reverse_rows(value):
    return dot(reversal(value.shape[0]), value).astype(value.dtype)


def reverse_both(value):
    return reverse_lanes(reverse_rows(value))


def call(kernel, out_shapes, *operands, scalars=0, scratch=(), flops=0, moved=0):
    specs = [pl.BlockSpec(memory_space=pltpu.SMEM)] * scalars
    specs += [pl.BlockSpec(memory_space=pltpu.VMEM)] * (len(operands) - scalars)
    return pl.pallas_call(
        kernel,
        out_shape=out_shapes,
        in_specs=specs,
        out_specs=[pl.BlockSpec(memory_space=pltpu.VMEM)] * len(out_shapes),
        scratch_shapes=list(scratch),
        cost_estimate=pl.CostEstimate(flops=flops, bytes_accessed=moved, transcendentals=0),
        compiler_params=pltpu.CompilerParams(vmem_limit_bytes=48 * 1024 * 1024),
    )(*operands)


def token_row(ids_ref, mask_ref, strand):
    return jnp.where(mask_ref[strand] == 1, 5, ids_ref[strand]).astype(F32)


def lead_kernel(
    normed_ref, grad_ref, ids_ref, mask_ref, send_ref, tails_ref, heads_ref, far_ref,
    head, ids, mask, arrived,
):
    rows, width = send_ref.shape
    copies = [
        pltpu.make_async_copy(source, target, arrived.at[place])
        for place, (source, target) in enumerate(
            (
                (normed_ref.at[1], send_ref),
                (normed_ref.at[:, rows - HALO : rows, :], tails_ref),
                (grad_ref.at[:, 0:HALO, :], head),
                (grad_ref.at[1], far_ref),
                (ids_ref, ids),
                (mask_ref, mask),
            )
        )
    ]
    for copy in copies:
        copy.start()
    for copy in copies:
        copy.wait()
    at_row = lax.broadcasted_iota(jnp.int32, (HALO, width), 0) == HALO - 1
    for strand in range(2):
        tokens = token_row(ids, mask, strand)
        tokens = jnp.concatenate([tokens, jnp.zeros((1, width - LANES), F32)], axis=1)
        heads_ref[strand] = jnp.where(at_row, tokens, head[strand].astype(F32)).astype(BF16)


def flip_kernel(grad_ref, out_ref):
    out_ref[...] = reverse_both(grad_ref[...])


def edge_kernel(ids_ref, mask_ref, tails_ref, heads_ref, slab_ref):
    width = slab_ref.shape[1]
    head = heads_ref[1].astype(F32)
    swap = reversal(HALO, F32)
    tail_rev = jnp.dot(swap, tails_ref[1].astype(F32), preferred_element_type=F32).astype(BF16)
    head_rev = jnp.dot(swap, head, preferred_element_type=F32).astype(BF16)
    own = token_row(ids_ref, mask_ref, 1)
    both = jnp.concatenate([own, head[HALO - 1 : HALO, :LANES], jnp.zeros((6, LANES), F32)], axis=0)
    flipped = dot(both.astype(BF16), reversal(LANES))
    tokens = jnp.concatenate([flipped[0:1], flipped[1:2], jnp.zeros((1, width - 2 * LANES), F32)], axis=1)
    at_row = lax.broadcasted_iota(jnp.int32, (HALO, width), 0) == HALO - 1
    slab_ref[0:HALO, :] = reverse_lanes(head_rev)
    slab_ref[HALO:, :] = jnp.where(at_row, tokens, reverse_lanes(tail_rev).astype(F32)).astype(BF16)


def forward_kernel(place_ref, own_ref, near_ref, other_ref, normed_ref, tails_ref, weight_ref, values_ref):
    shard = own_ref.shape[0]
    half = 4 * shard
    x_lo = place_ref[0] // 2
    core = place_ref[0] % 2
    pieces = (
        (own_ref[...], x_lo, core),
        (near_ref[...], 1 - x_lo, core),
        (other_ref[0:shard, :], x_lo, 1 - core),
        (other_ref[shard:, :], 1 - x_lo, 1 - core),
    )
    for block, chip, at_core in pieces:
        index = chip * 2 + at_core
        weight_ref[pl.ds(pl.multiple_of(index * shard, shard), shard), :] = block
        back = half + (3 - index) * shard
        weight_ref[pl.ds(pl.multiple_of(back, shard), shard), :] = reverse_both(block)
    weight = weight_ref[...]
    values_ref[HALO:, :] = dot(normed_ref[0], weight).astype(BF16).astype(F32)
    values_ref[0:HALO, :] = dot(tails_ref[0], weight).astype(BF16).astype(F32)


def one_hot(row, count):
    classes = lax.broadcasted_iota(jnp.int32, (HALO, count), 0)
    return (row.astype(jnp.int32) == classes).astype(F32)


def rows_of(hot, table):
    return lax.dot_general(
        hot, table, (((0,), (0,)), ((), ())), preferred_element_type=F32, precision=HIGHEST
    )


def near_strand_kernel(
    far_ref, weight_ref, values0_ref, grad_ref, ids_ref, mask_ref, filter_ref, bias_ref,
    values1_ref, conv_grad_ref, mirror_ref, terms_ref,
):
    rows, width = grad_ref.shape[1], grad_ref.shape[2]
    taps = filter_ref.shape[0]
    values1_ref[...] = dot(reverse_both(far_ref[...]), weight_ref[...]).astype(BF16).astype(F32)
    hot = one_hot(token_row(ids_ref, mask_ref, 0), LANES)
    wide = 2 * LANES
    for index in range(width // wide):
        cols = slice(index * wide, (index + 1) * wide)
        weights = filter_ref[:, cols]
        own = grad_ref[0, :, cols].astype(F32)
        gate = jax.nn.sigmoid(values1_ref[:, cols] + rows_of(hot, bias_ref[:, cols]))
        conv_grad = own * gate
        conv_grad_ref[:, cols] = conv_grad
        conv = jnp.zeros((rows, wide), F32)
        for tap in range(taps):
            shifted = values0_ref[HALO - tap : HALO - tap + rows, cols]
            conv = conv + weights[tap : tap + 1] * shifted
            terms_ref[tap : tap + 1, cols] = jnp.sum(conv_grad * shifted, axis=0, keepdims=True)
        pre = own * conv * gate * (1.0 - gate)
        mirror_ref[:, cols] = pre.astype(BF16)
        terms_ref[8:16, cols] = jnp.dot(hot, pre, preferred_element_type=F32, precision=HIGHEST)
    terms_ref[7:8, :] = jnp.zeros((1, width), F32)


def far_strand_kernel(
    slab_ref, halo_ref, weight_ref, values0_ref, values1_ref, mirror_ref, heads_ref,
    filter_rev_ref, bias_ref, bias_rev_ref,
    send_ref, mirror_out_ref, edge_ref,
    wide1, pull1, sums,
):
    rows, width = mirror_ref.shape
    taps = filter_rev_ref.shape[0]
    tokens = halo_ref[HALO:, :].astype(F32)[HALO - 1 : HALO, :]
    hot_own = one_hot(tokens[:, :LANES], LANES)
    hot_far = one_hot(tokens[:, LANES : 2 * LANES], LANES)
    hot_edge = one_hot(heads_ref[0].astype(F32)[HALO - 1 : HALO, :LANES], LANES)
    edge = dot(halo_ref[HALO:, :], weight_ref[...]).astype(BF16).astype(F32)
    edge_gate = jax.nn.sigmoid(edge + rows_of(hot_edge, bias_ref[...])[0:HALO])
    edge_ref[...] = heads_ref[0].astype(F32) * edge_gate
    sums[...] = jnp.zeros_like(sums)
    wide = 2 * LANES
    for index in range(width // wide):
        cols = slice(index * wide, (index + 1) * wide)
        weights = filter_rev_ref[:, cols]
        wide1[0:rows, :] = values1_ref[:, cols]
        wide1[rows:, :] = edge[:, cols]
        own = slab_ref[:, cols].astype(F32)
        gate = jax.nn.sigmoid(values0_ref[HALO:, cols] + rows_of(hot_own, bias_rev_ref[:, cols]))
        far_gate = jax.nn.sigmoid(
            values0_ref[0:HALO, cols] + rows_of(hot_far, bias_rev_ref[:, cols])[LANES - HALO :]
        )
        conv_grad = own * gate
        pull1[HALO:, :] = conv_grad
        pull1[0:HALO, :] = halo_ref[0:HALO, cols].astype(F32) * far_gate
        conv = jnp.zeros((rows, wide), F32)
        for tap in range(taps):
            shifted = wide1[tap : tap + rows, :]
            conv = conv + weights[tap : tap + 1] * shifted
            sums[tap : tap + 1, cols] = jnp.sum(conv_grad * shifted, axis=0, keepdims=True)
        pre = own * conv * gate * (1.0 - gate)
        mirror_out_ref[:, cols] = pre.astype(BF16)
        sums[8:16, cols] = jnp.dot(hot_own, pre, preferred_element_type=F32, precision=HIGHEST)
        total = mirror_ref[:, cols].astype(F32)
        for tap in range(taps):
            total = total + weights[tap : tap + 1] * pull1[HALO - tap : HALO - tap + rows, :]
        send_ref[0:rows, cols] = total.astype(BF16)
    send_ref[rows:, :] = sums[...].astype(BF16)


def operands_kernel(
    normed_ref, conv_grad_ref, edge_ref, mirror_ref, filter_ref, left_ref, right_ref, pull0,
):
    rows, width = conv_grad_ref.shape
    half = width // 2
    pull0[0:rows, :] = conv_grad_ref[...]
    pull0[rows:, :] = edge_ref[...]
    for strand in range(2):
        value = normed_ref[strand]
        left_ref[strand * rows : (strand + 1) * rows, :] = value[:, :half]
        left_ref[(2 + strand) * rows : (3 + strand) * rows, :] = reverse_both(value)[:, :half]
    wide = 2 * LANES
    for index in range(width // wide):
        cols = slice(index * wide, (index + 1) * wide)
        total = mirror_ref[:, cols].astype(F32)
        for tap in range(filter_ref.shape[0]):
            total = total + filter_ref[tap : tap + 1, cols] * pull0[tap : tap + rows, cols]
        right_ref[0:rows, cols] = total.astype(BF16)
    right_ref[rows:, :] = reverse_both(right_ref[0:rows, :])


def project_kernel(
    place_ref, scale, left_ref, right_ref, back_ref, terms_ref,
    send_ref, keep_ref, sums_ref, final_ref,
):
    rows = right_ref.shape[0] // 2
    back = back_ref[0:rows, :]
    home = reverse_both(back)
    final_ref[0] = right_ref[0:rows, :]
    final_ref[1] = home
    right = jnp.concatenate([right_ref[0:rows, :], home, right_ref[rows:, :], back], axis=0)
    sums = (terms_ref[...] + reverse_lanes(back_ref[rows:, :]).astype(F32)) * scale
    sums_ref[...] = sums
    core = place_ref[0] % 2
    shard = left_ref.shape[1] // 4
    for chip in range(2):
        for mine in range(2):
            index = chip * 2 + (core if mine else 1 - core)
            left = left_ref[:, pl.ds(pl.multiple_of(index * shard, shard), shard)]
            part = lax.dot_general(left, right, (((0,), (0,)), ((), ())), preferred_element_type=F32) * scale
            if mine:
                keep_ref[chip * shard : (chip + 1) * shard, :] = part
            else:
                send_ref[chip * shard : (chip + 1) * shard, :] = part.astype(BF16)
    send_ref[2 * shard :, :] = sums.astype(BF16)


def input_grad_kernel(value_grad_ref, weight_ref, out_ref):
    weight = weight_ref[...]
    for strand in range(2):
        out_ref[strand] = lax.dot_general(
            value_grad_ref[strand], weight, (((1,), (1,)), ((), ())), preferred_element_type=F32
        ).astype(BF16)


def first_sum_kernel(place_ref, keep_ref, got_ref, sums_ref, send_ref, keep_out_ref, sums_out_ref):
    shard = keep_ref.shape[0] // 2
    x_lo = place_ref[0] // 2
    here = pl.ds(pl.multiple_of(x_lo * shard, shard), shard)
    there = pl.ds(pl.multiple_of((1 - x_lo) * shard, shard), shard)
    keep_out_ref[...] = keep_ref[here, :] + got_ref[here, :].astype(F32)
    send_ref[0:shard, :] = (keep_ref[there, :] + got_ref[there, :].astype(F32)).astype(BF16)
    sums = sums_ref[...] + got_ref[2 * shard :, :].astype(F32)
    sums_out_ref[...] = sums
    send_ref[shard:, :] = sums.astype(BF16)


def last_sum_kernel(place_ref, keep_ref, got_ref, sums_ref, proj_ref, filter_ref, bias_ref):
    shard = keep_ref.shape[0]
    part = filter_ref.shape[2]
    proj_ref[...] = keep_ref[...] + got_ref[0:shard, :].astype(F32)
    cols = pl.ds(pl.multiple_of(place_ref[0] * part, part), part)
    sums = sums_ref[:, cols] + got_ref[shard:, cols].astype(F32)
    for tap in range(filter_ref.shape[0]):
        filter_ref[tap] = sums[tap : tap + 1, :]
    for token in range(bias_ref.shape[0]):
        bias_ref[token] = sums[8 + token : 9 + token, :]


def mirrored(value):
    size = lax.axis_size("ctx")
    return lax.ppermute(value, "ctx", [(i, size - 1 - i) for i in range(size)])


def shifted(value, distance):
    devices = range(lax.axis_size("ctx"))
    return lax.ppermute(value, "ctx", [(i, i + distance) for i in devices if i + distance in devices])


def partner(value, bit):
    return lax.ppermute(value, "fsdp", [(i, i ^ bit) for i in range(lax.axis_size("fsdp"))])


def shape(dims, dtype):
    return jax.ShapeDtypeStruct(dims, dtype)


def step(normed, out_grad, ids, mask, proj_half, conv_filter, gate_bias):
    rows, width = normed.shape[2], normed.shape[3]
    taps = conv_filter.shape[0]
    shard = proj_half.shape[0]
    classes = gate_bias.shape[0]
    normed, out_grad = normed[:, 0], out_grad[:, 0]
    place = lax.axis_index("fsdp").astype(jnp.int32).reshape(1)

    send, tails, heads, far_grad = pl.pallas_call(
        lead_kernel,
        out_shape=(
            shape((rows, width), BF16),
            shape((2, HALO, width), BF16),
            shape((2, HALO, width), BF16),
            shape((rows, width), BF16),
        ),
        in_specs=[pl.BlockSpec(memory_space=pltpu.HBM)] * 4,
        out_specs=[pl.BlockSpec(memory_space=pltpu.VMEM)] * 4,
        scratch_shapes=[
            pltpu.VMEM((2, HALO, width), BF16),
            pltpu.VMEM((2, 1, rows), jnp.int32),
            pltpu.VMEM((2, 1, rows), jnp.int32),
            pltpu.SemaphoreType.DMA((6,)),
        ],
        cost_estimate=pl.CostEstimate(flops=0, bytes_accessed=4 * rows * width, transcendentals=0),
    )(normed, out_grad, ids, mask)
    normed_far = mirrored(send)
    heads = shifted(heads, -1)
    tails = shifted(tails, 1)
    far_grad, = call(
        flip_kernel, (shape((rows, width), BF16),), far_grad, flops=600 * rows * width, moved=4 * rows * width,
    )
    slab = mirrored(far_grad)
    near = partner(proj_half, 2)
    halo, = call(
        edge_kernel, (shape((2 * HALO, width), BF16),), ids, mask, tails, heads,
        flops=600 * HALO * width, moved=8 * HALO * width,
    )
    halo = mirrored(halo)
    other = partner(jnp.concatenate([proj_half, near], axis=0), 1)
    filter_rev = conv_filter[:, ::-1]
    bias = jnp.pad(gate_bias, ((0, HALO - classes), (0, 0)))
    bias_rev = bias[:, ::-1]

    weight, values0 = call(
        forward_kernel,
        (shape((width, width), BF16), shape((rows + HALO, width), F32)),
        place, proj_half, near, other, normed, tails, scalars=1,
        flops=2 * rows * width * width, moved=6 * width * width,
    )
    values1, conv_grad, mirror0, terms = call(
        near_strand_kernel,
        (
            shape((rows, width), F32),
            shape((rows, width), F32),
            shape((rows, width), BF16),
            shape((16, width), F32),
        ),
        normed_far, weight, values0, out_grad, ids, mask, conv_filter, bias,
        flops=2 * rows * width * width, moved=8 * width * width,
    )
    wide = 2 * LANES
    send, mirror1, edge = call(
        far_strand_kernel,
        (shape((rows + 16, width), BF16), shape((rows, width), BF16), shape((HALO, width), F32)),
        slab, halo, weight, values0, values1, mirror0, heads, filter_rev, bias, bias_rev,
        scratch=[pltpu.VMEM((rows + HALO, wide), F32)] * 2 + [pltpu.VMEM((16, width), F32)],
        flops=2 * rows * width * width, moved=8 * width * width,
    )
    back = mirrored(send)
    left, right = call(
        operands_kernel, (shape((4 * rows, width // 2), BF16), shape((2 * rows, width), BF16)),
        normed, conv_grad, edge, mirror1, conv_filter,
        scratch=[pltpu.VMEM((rows + HALO, width), F32)],
        flops=rows * width * width, moved=16 * rows * width,
    )
    grad_scale = 1.0 / math.sqrt(2.0 * lax.axis_size("fsdp") * rows)
    send1, keep1, sums1, final = call(
        lambda place_ref, *refs: project_kernel(place_ref, grad_scale, *refs),
        (
            shape((2 * shard + 16, width), BF16),
            shape((2 * shard, width), F32),
            shape((16, width), F32),
            shape((2, rows, width), BF16),
        ),
        place, left, right, back, terms, scalars=1,
        flops=4 * rows * width * width, moved=4 * width * width,
    )
    got1 = partner(send1, 1)
    send2, keep2, sums2 = call(
        first_sum_kernel,
        (shape((shard + 16, width), BF16), shape((shard, width), F32), shape((16, width), F32)),
        place, keep1, got1, sums1, scalars=1, moved=16 * shard * width,
    )
    got2 = partner(send2, 2)
    in_grad, = call(
        input_grad_kernel, (shape((2, rows, width), BF16),), final, weight,
        flops=4 * rows * width * width, moved=4 * width * width,
    )
    part = width // lax.axis_size("fsdp")
    proj_grad, filter_grad, bias_grad = call(
        last_sum_kernel,
        (shape((shard, width), F32), shape((taps, 1, part), F32), shape((classes, 1, part), F32)),
        place, keep2, got2, sums2, scalars=1, moved=12 * shard * width,
    )
    return (
        in_grad[:, None],
        proj_grad[None],
        jnp.transpose(filter_grad, (1, 0, 2)),
        jnp.transpose(bias_grad, (1, 0, 2)),
    )


def solution(mesh):
    placed = (
        P(None, "fsdp", "ctx", None),
        P(None, "fsdp", "ctx", None),
        P(None, "fsdp", "ctx"),
        P(None, "fsdp", "ctx"),
        P("fsdp", None),
        P(),
        P(),
    )
    return jax.shard_map(
        step,
        mesh=mesh,
        in_specs=placed,
        out_specs=(
            P(None, "fsdp", "ctx", None),
            P("ctx", "fsdp", None),
            P("ctx", None, "fsdp"),
            P("ctx", None, "fsdp"),
        ),
        check_vma=False,
    )
```

```python
import functools
import math

import jax
import jax.numpy as jnp
from jax import lax
from jax.experimental import pallas as pl
from jax.experimental.pallas import tpu as pltpu
from jax.sharding import PartitionSpec as P


LANES = 128
HALO = 8
F32 = jnp.float32
BF16 = jnp.bfloat16
HIGHEST = lax.Precision.HIGHEST


def dot(a, b):
    return jnp.dot(a, b, preferred_element_type=F32)


def reversal(size, dtype=BF16):
    rows = lax.broadcasted_iota(jnp.int32, (size, size), 0)
    cols = lax.broadcasted_iota(jnp.int32, (size, size), 1)
    return (rows + cols == size - 1).astype(dtype)


def reverse_lanes(value, precision=None):
    count = value.shape[-1] // LANES
    swap = reversal(LANES, value.dtype)
    parts = []
    for block in reversed(range(count)):
        part = value[:, block * LANES : (block + 1) * LANES]
        parts.append(
            jnp.dot(part, swap, preferred_element_type=F32, precision=precision).astype(value.dtype)
        )
    return jnp.concatenate(parts, axis=1)


def reverse_rows(value):
    return dot(reversal(value.shape[0]), value).astype(value.dtype)


def reverse_both(value):
    return reverse_lanes(reverse_rows(value))


def call(kernel, out_shapes, *operands, scalars=0, scratch=(), flops=0, moved=0):
    specs = [pl.BlockSpec(memory_space=pltpu.SMEM)] * scalars
    specs += [pl.BlockSpec(memory_space=pltpu.VMEM)] * (len(operands) - scalars)
    return pl.pallas_call(
        kernel,
        out_shape=out_shapes,
        in_specs=specs,
        out_specs=[pl.BlockSpec(memory_space=pltpu.VMEM)] * len(out_shapes),
        scratch_shapes=list(scratch),
        cost_estimate=pl.CostEstimate(flops=flops, bytes_accessed=moved, transcendentals=0),
        compiler_params=pltpu.CompilerParams(vmem_limit_bytes=48 * 1024 * 1024),
    )(*operands)


def token_row(ids_ref, mask_ref, strand):
    return jnp.where(mask_ref[strand] == 1, 5, ids_ref[strand]).astype(F32)


def lead_kernel(
    normed_ref, grad_ref, ids_ref, mask_ref, send_ref, tails_ref, heads_ref, far_ref,
    head, ids, mask, arrived,
):
    rows, width = send_ref.shape
    copies = [
        pltpu.make_async_copy(source, target, arrived.at[place])
        for place, (source, target) in enumerate(
            (
                (normed_ref.at[1], send_ref),
                (normed_ref.at[:, rows - HALO : rows, :], tails_ref),
                (grad_ref.at[:, 0:HALO, :], head),
                (grad_ref.at[1], far_ref),
                (ids_ref, ids),
                (mask_ref, mask),
            )
        )
    ]
    for copy in copies:
        copy.start()
    for copy in copies:
        copy.wait()
    at_row = lax.broadcasted_iota(jnp.int32, (HALO, width), 0) == HALO - 1
    for strand in range(2):
        tokens = token_row(ids, mask, strand)
        tokens = jnp.concatenate([tokens, jnp.zeros((1, width - LANES), F32)], axis=1)
        heads_ref[strand] = jnp.where(at_row, tokens, head[strand].astype(F32)).astype(BF16)


def spans_of(chunk, width):
    part = width // 4
    starts = (0, 3 * part) if chunk == 0 else (part, 2 * part)
    return [
        (slice(start, start + part), slice(place * part, (place + 1) * part))
        for place, start in enumerate(starts)
    ]


def flip_kernel(grad_ref, *out_refs):
    whole = reverse_both(grad_ref[...])
    for chunk, out_ref in enumerate(out_refs):
        for cols, own in spans_of(chunk, whole.shape[1]):
            out_ref[:, own] = whole[:, cols]


def edge_kernel(ids_ref, mask_ref, tails_ref, heads_ref, slab_ref):
    width = slab_ref.shape[1]
    head = heads_ref[1].astype(F32)
    swap = reversal(HALO, F32)
    tail_rev = jnp.dot(swap, tails_ref[1].astype(F32), preferred_element_type=F32).astype(BF16)
    head_rev = jnp.dot(swap, head, preferred_element_type=F32).astype(BF16)
    own = token_row(ids_ref, mask_ref, 1)
    both = jnp.concatenate([own, head[HALO - 1 : HALO, :LANES], jnp.zeros((6, LANES), F32)], axis=0)
    flipped = dot(both.astype(BF16), reversal(LANES))
    tokens = jnp.concatenate([flipped[0:1], flipped[1:2], jnp.zeros((1, width - 2 * LANES), F32)], axis=1)
    at_row = lax.broadcasted_iota(jnp.int32, (HALO, width), 0) == HALO - 1
    slab_ref[0:HALO, :] = reverse_lanes(head_rev)
    slab_ref[HALO:, :] = jnp.where(at_row, tokens, reverse_lanes(tail_rev).astype(F32)).astype(BF16)


def forward_kernel(place_ref, own_ref, near_ref, other_ref, normed_ref, tails_ref, weight_ref, values_ref):
    shard = own_ref.shape[0]
    half = 4 * shard
    x_lo = place_ref[0] // 2
    core = place_ref[0] % 2
    pieces = (
        (own_ref[...], x_lo, core),
        (near_ref[...], 1 - x_lo, core),
        (other_ref[0:shard, :], x_lo, 1 - core),
        (other_ref[shard:, :], 1 - x_lo, 1 - core),
    )
    for block, chip, at_core in pieces:
        index = chip * 2 + at_core
        weight_ref[pl.ds(pl.multiple_of(index * shard, shard), shard), :] = block
        back = half + (3 - index) * shard
        weight_ref[pl.ds(pl.multiple_of(back, shard), shard), :] = reverse_both(block)
    weight = weight_ref[...]
    values_ref[HALO:, :] = dot(normed_ref[0], weight).astype(BF16).astype(F32)
    values_ref[0:HALO, :] = dot(tails_ref[0], weight).astype(BF16).astype(F32)


def one_hot(row, count):
    classes = lax.broadcasted_iota(jnp.int32, (HALO, count), 0)
    return (row.astype(jnp.int32) == classes).astype(F32)


def rows_of(hot, table):
    return lax.dot_general(
        hot, table, (((0,), (0,)), ((), ())), preferred_element_type=F32, precision=HIGHEST
    )


def near_strand_kernel(
    far_ref, weight_ref, values0_ref, grad_ref, ids_ref, mask_ref, filter_ref, bias_ref,
    values1_ref, conv_grad_ref, mirror_ref, terms_ref,
):
    rows, width = grad_ref.shape[1], grad_ref.shape[2]
    taps = filter_ref.shape[0]
    values1_ref[...] = dot(reverse_both(far_ref[...]), weight_ref[...]).astype(BF16).astype(F32)
    hot = one_hot(token_row(ids_ref, mask_ref, 0), LANES)
    wide = 2 * LANES
    for index in range(width // wide):
        cols = slice(index * wide, (index + 1) * wide)
        weights = filter_ref[:, cols]
        own = grad_ref[0, :, cols].astype(F32)
        gate = jax.nn.sigmoid(values1_ref[:, cols] + rows_of(hot, bias_ref[:, cols]))
        conv_grad = own * gate
        conv_grad_ref[:, cols] = conv_grad
        conv = jnp.zeros((rows, wide), F32)
        for tap in range(taps):
            shifted = values0_ref[HALO - tap : HALO - tap + rows, cols]
            conv = conv + weights[tap : tap + 1] * shifted
            terms_ref[tap : tap + 1, cols] = jnp.sum(conv_grad * shifted, axis=0, keepdims=True)
        pre = own * conv * gate * (1.0 - gate)
        mirror_ref[:, cols] = pre.astype(BF16)
        terms_ref[8:16, cols] = jnp.dot(hot, pre, preferred_element_type=F32, precision=HIGHEST)
    terms_ref[7:8, :] = jnp.zeros((1, width), F32)


def far_strand_kernel(
    chunk, slab_ref, halo_ref, weight_ref, values0_ref, values1_ref, mirror_ref, heads_ref,
    filter_rev_ref, bias_ref, bias_rev_ref,
    send_ref, mirror_out_ref, edge_ref,
    wide1, pull1, sums,
):
    rows, width = mirror_ref.shape
    taps = filter_rev_ref.shape[0]
    tokens = halo_ref[HALO:, :].astype(F32)[HALO - 1 : HALO, :]
    hot_own = one_hot(tokens[:, :LANES], LANES)
    hot_far = one_hot(tokens[:, LANES : 2 * LANES], LANES)
    hot_edge = one_hot(heads_ref[0].astype(F32)[HALO - 1 : HALO, :LANES], LANES)
    sums[...] = jnp.zeros_like(sums)
    for cols, local in spans_of(chunk, width):
        edge = dot(halo_ref[HALO:, :], weight_ref[:, cols]).astype(BF16).astype(F32)
        edge_gate = jax.nn.sigmoid(edge + rows_of(hot_edge, bias_ref[:, cols])[0:HALO])
        edge_ref[:, local] = heads_ref[0, :, cols].astype(F32) * edge_gate
        weights = filter_rev_ref[:, cols]
        wide1[0:rows, :] = values1_ref[:, cols]
        wide1[rows:, :] = edge
        own = slab_ref[:, local].astype(F32)
        gate = jax.nn.sigmoid(values0_ref[HALO:, cols] + rows_of(hot_own, bias_rev_ref[:, cols]))
        far_gate = jax.nn.sigmoid(
            values0_ref[0:HALO, cols] + rows_of(hot_far, bias_rev_ref[:, cols])[LANES - HALO :]
        )
        conv_grad = own * gate
        pull1[HALO:, :] = conv_grad
        pull1[0:HALO, :] = halo_ref[0:HALO, cols].astype(F32) * far_gate
        conv = jnp.zeros_like(own)
        for tap in range(taps):
            shifted = wide1[tap : tap + rows, :]
            conv = conv + weights[tap : tap + 1] * shifted
            sums[tap : tap + 1, local] = jnp.sum(conv_grad * shifted, axis=0, keepdims=True)
        pre = own * conv * gate * (1.0 - gate)
        mirror_out_ref[:, local] = pre.astype(BF16)
        sums[8:16, local] = jnp.dot(hot_own, pre, preferred_element_type=F32, precision=HIGHEST)
        total = mirror_ref[:, cols].astype(F32)
        for tap in range(taps):
            total = total + weights[tap : tap + 1] * pull1[HALO - tap : HALO - tap + rows, :]
        send_ref[0:rows, local] = total.astype(BF16)
    send_ref[rows:, :] = sums[...].astype(BF16)


def left_kernel(normed_ref, left_ref):
    rows = normed_ref.shape[1]
    half = normed_ref.shape[2] // 2
    for strand in range(2):
        value = normed_ref[strand]
        left_ref[strand * rows : (strand + 1) * rows, :] = value[:, :half]
        left_ref[(2 + strand) * rows : (3 + strand) * rows, :] = reverse_both(value)[:, :half]


def near_grad_kernel(chunk, conv_grad_ref, edge_ref, mirror_ref, filter_ref, right_ref, pull0):
    rows, width = conv_grad_ref.shape
    for cols, local in spans_of(chunk, width):
        pull0[0:rows, :] = conv_grad_ref[:, cols]
        pull0[rows:, :] = edge_ref[:, local]
        total = mirror_ref[:, local].astype(F32)
        for tap in range(filter_ref.shape[0]):
            total = total + filter_ref[tap : tap + 1, cols] * pull0[tap : tap + rows, :]
        right_ref[0:rows, local] = total.astype(BF16)
    right_ref[rows:, :] = reverse_both(right_ref[0:rows, :])


def project_kernel(
    chunk, scale, place_ref, left_ref, right_ref, back_ref, terms_ref,
    send_ref, keep_ref, sums_ref, final_ref,
):
    rows = right_ref.shape[0] // 2
    back = back_ref[0:rows, :]
    home = reverse_both(back)
    final_ref[0] = right_ref[0:rows, :]
    final_ref[1] = home
    right = jnp.concatenate([right_ref[0:rows, :], home, right_ref[rows:, :], back], axis=0)
    terms = jnp.concatenate([terms_ref[:, cols] for cols, _ in spans_of(chunk, terms_ref.shape[1])], axis=1)
    sums = (terms + reverse_lanes(back_ref[rows:, :]).astype(F32)) * scale
    sums_ref[...] = sums
    core = place_ref[0] % 2
    shard = left_ref.shape[1] // 4
    for chip in range(2):
        for mine in range(2):
            index = chip * 2 + (core if mine else 1 - core)
            left = left_ref[:, pl.ds(pl.multiple_of(index * shard, shard), shard)]
            part = lax.dot_general(left, right, (((0,), (0,)), ((), ())), preferred_element_type=F32) * scale
            if mine:
                keep_ref[chip * shard : (chip + 1) * shard, :] = part
            else:
                send_ref[chip * shard : (chip + 1) * shard, :] = part.astype(BF16)
    send_ref[2 * shard :, :] = sums.astype(BF16)


def input_grad_kernel(outer_ref, inner_ref, weight_ref, out_ref):
    weight = weight_ref[...]
    part = weight.shape[1] // 4
    for strand in range(2):
        outer = outer_ref[strand]
        value = jnp.concatenate([outer[:, :part], inner_ref[strand], outer[:, part:]], axis=1)
        out_ref[strand] = lax.dot_general(
            value, weight, (((1,), (1,)), ((), ())), preferred_element_type=F32
        ).astype(BF16)


def first_sum_kernel(place_ref, keep_ref, got_ref, sums_ref, send_ref, keep_out_ref, sums_out_ref):
    shard = keep_ref.shape[0] // 2
    x_lo = place_ref[0] // 2
    here = pl.ds(pl.multiple_of(x_lo * shard, shard), shard)
    there = pl.ds(pl.multiple_of((1 - x_lo) * shard, shard), shard)
    keep_out_ref[...] = keep_ref[here, :] + got_ref[here, :].astype(F32)
    send_ref[0:shard, :] = (keep_ref[there, :] + got_ref[there, :].astype(F32)).astype(BF16)
    sums = sums_ref[...] + got_ref[2 * shard :, :].astype(F32)
    sums_out_ref[...] = sums
    send_ref[shard:, :] = sums.astype(BF16)


def last_sum_kernel(
    place_ref, keep0_ref, got0_ref, sums0_ref, keep1_ref, got1_ref, sums1_ref,
    proj_ref, filter_ref, bias_ref,
):
    shard, width = proj_ref.shape
    part = filter_ref.shape[2]
    place = place_ref[0]
    picked = []
    for chunk, (keep_ref, got_ref, sums_ref) in enumerate(
        ((keep0_ref, got0_ref, sums0_ref), (keep1_ref, got1_ref, sums1_ref))
    ):
        for cols, local in spans_of(chunk, width):
            proj_ref[:, cols] = keep_ref[:, local] + got_ref[0:shard, local].astype(F32)
        mine = pl.ds(pl.multiple_of((place // 2) * part, part), part)
        picked.append(sums_ref[:, mine] + got_ref[shard:, mine].astype(F32))
    inner = jnp.logical_or(place == 1, place == 2)
    sums = jnp.where(inner, picked[1], picked[0])
    for tap in range(filter_ref.shape[0]):
        filter_ref[tap] = sums[tap : tap + 1, :]
    for token in range(bias_ref.shape[0]):
        bias_ref[token] = sums[8 + token : 9 + token, :]


def mirrored(value):
    size = lax.axis_size("ctx")
    return lax.ppermute(value, "ctx", [(i, size - 1 - i) for i in range(size)])


def shifted(value, distance):
    devices = range(lax.axis_size("ctx"))
    return lax.ppermute(value, "ctx", [(i, i + distance) for i in devices if i + distance in devices])


def partner(value, bit):
    return lax.ppermute(value, "fsdp", [(i, i ^ bit) for i in range(lax.axis_size("fsdp"))])


def shape(dims, dtype):
    return jax.ShapeDtypeStruct(dims, dtype)


def step(normed, out_grad, ids, mask, proj_half, conv_filter, gate_bias):
    rows, width = normed.shape[2], normed.shape[3]
    taps = conv_filter.shape[0]
    shard = proj_half.shape[0]
    classes = gate_bias.shape[0]
    normed, out_grad = normed[:, 0], out_grad[:, 0]
    place = lax.axis_index("fsdp").astype(jnp.int32).reshape(1)

    send, tails, heads, far_grad = pl.pallas_call(
        lead_kernel,
        out_shape=(
            shape((rows, width), BF16),
            shape((2, HALO, width), BF16),
            shape((2, HALO, width), BF16),
            shape((rows, width), BF16),
        ),
        in_specs=[pl.BlockSpec(memory_space=pltpu.HBM)] * 4,
        out_specs=[pl.BlockSpec(memory_space=pltpu.VMEM)] * 4,
        scratch_shapes=[
            pltpu.VMEM((2, HALO, width), BF16),
            pltpu.VMEM((2, 1, rows), jnp.int32),
            pltpu.VMEM((2, 1, rows), jnp.int32),
            pltpu.SemaphoreType.DMA((6,)),
        ],
        cost_estimate=pl.CostEstimate(flops=0, bytes_accessed=4 * rows * width, transcendentals=0),
    )(normed, out_grad, ids, mask)
    normed_far = mirrored(send)
    heads = shifted(heads, -1)
    tails = shifted(tails, 1)
    half = width // 2
    far_grads = call(
        flip_kernel, (shape((rows, half), BF16),) * 2, far_grad, flops=600 * rows * width, moved=4 * rows * width,
    )
    slabs = [mirrored(far) for far in far_grads]
    near = partner(proj_half, 2)
    halo, = call(
        edge_kernel, (shape((2 * HALO, width), BF16),), ids, mask, tails, heads,
        flops=600 * HALO * width, moved=8 * HALO * width,
    )
    halo = mirrored(halo)
    other = partner(jnp.concatenate([proj_half, near], axis=0), 1)
    filter_rev = conv_filter[:, ::-1]
    bias = jnp.pad(gate_bias, ((0, HALO - classes), (0, 0)))
    bias_rev = bias[:, ::-1]

    weight, values0 = call(
        forward_kernel,
        (shape((width, width), BF16), shape((rows + HALO, width), F32)),
        place, proj_half, near, other, normed, tails, scalars=1,
        flops=2 * rows * width * width, moved=6 * width * width,
    )
    values1, conv_grad, mirror0, terms = call(
        near_strand_kernel,
        (
            shape((rows, width), F32),
            shape((rows, width), F32),
            shape((rows, width), BF16),
            shape((16, width), F32),
        ),
        normed_far, weight, values0, out_grad, ids, mask, conv_filter, bias,
        flops=2 * rows * width * width, moved=8 * width * width,
    )
    left, = call(left_kernel, (shape((4 * rows, half), BF16),), normed, flops=rows * width * width)
    grad_scale = 1.0 / math.sqrt(2.0 * lax.axis_size("fsdp") * rows)
    part = width // lax.axis_size("fsdp")
    chunks = []
    for chunk in range(2):
        window = pltpu.VMEM((rows + HALO, part), F32)
        send, mirror1, edge = call(
            functools.partial(far_strand_kernel, chunk),
            (shape((rows + 16, half), BF16), shape((rows, half), BF16), shape((HALO, half), F32)),
            slabs[chunk], halo, weight, values0, values1, mirror0, heads, filter_rev, bias, bias_rev,
            scratch=[window, window, pltpu.VMEM((16, half), F32)],
            flops=rows * width * width, moved=4 * width * width,
        )
        back = mirrored(send)
        right, = call(
            functools.partial(near_grad_kernel, chunk), (shape((2 * rows, half), BF16),),
            conv_grad, edge, mirror1, conv_filter,
            scratch=[window], flops=rows * width * width // 2, moved=8 * rows * width,
        )
        chunks.append((back, right))
    sums = []
    finals = []
    for chunk, (back, right) in enumerate(chunks):
        send1, keep1, sums1, final = call(
            functools.partial(project_kernel, chunk, grad_scale),
            (
                shape((2 * shard + 16, half), BF16),
                shape((2 * shard, half), F32),
                shape((16, half), F32),
                shape((2, rows, half), BF16),
            ),
            place, left, right, back, terms, scalars=1,
            flops=2 * rows * width * width, moved=2 * width * width,
        )
        finals.append(final)
        got1 = partner(send1, 1)
        send2, keep2, sums2 = call(
            first_sum_kernel,
            (shape((shard + 16, half), BF16), shape((shard, half), F32), shape((16, half), F32)),
            place, keep1, got1, sums1, scalars=1, moved=8 * shard * width,
        )
        got2 = partner(send2, 2)
        sums += [keep2, got2, sums2]
    in_grad, = call(
        input_grad_kernel, (shape((2, rows, width), BF16),), *finals, weight,
        flops=4 * rows * width * width, moved=4 * width * width,
    )
    proj_grad, filter_grad, bias_grad = call(
        last_sum_kernel,
        (shape((shard, width), F32), shape((taps, 1, part), F32), shape((classes, 1, part), F32)),
        place, *sums, scalars=1, moved=12 * shard * width,
    )
    return (
        in_grad[:, None],
        proj_grad[None],
        jnp.transpose(filter_grad, (1, 0, 2)),
        jnp.transpose(bias_grad, (1, 0, 2)),
    )


def solution(mesh):
    placed = (
        P(None, "fsdp", "ctx", None),
        P(None, "fsdp", "ctx", None),
        P(None, "fsdp", "ctx"),
        P(None, "fsdp", "ctx"),
        P("fsdp", None),
        P(),
        P(),
    )
    return jax.shard_map(
        step,
        mesh=mesh,
        in_specs=placed,
        out_specs=(
            P(None, "fsdp", "ctx", None),
            P("ctx", "fsdp", None),
            P("ctx", None, "fsdp"),
            P("ctx", None, "fsdp"),
        ),
        check_vma=False,
    )
```

```python
import functools
import math

import jax
import jax.numpy as jnp
from jax import lax
from jax.experimental import pallas as pl
from jax.experimental.pallas import tpu as pltpu
from jax.sharding import PartitionSpec as P


LANES = 128
HALO = 8
PLANE = 8
F32 = jnp.float32
BF16 = jnp.bfloat16
HIGHEST = lax.Precision.HIGHEST


def dot(a, b):
    return jnp.dot(a, b, preferred_element_type=F32)


def reversal(size, dtype=BF16):
    rows = lax.broadcasted_iota(jnp.int32, (size, size), 0)
    cols = lax.broadcasted_iota(jnp.int32, (size, size), 1)
    return (rows + cols == size - 1).astype(dtype)


def reverse_lanes(value, precision=None):
    count = value.shape[-1] // LANES
    swap = reversal(LANES, value.dtype)
    parts = []
    for block in reversed(range(count)):
        part = value[:, block * LANES : (block + 1) * LANES]
        parts.append(
            jnp.dot(part, swap, preferred_element_type=F32, precision=precision).astype(value.dtype)
        )
    return jnp.concatenate(parts, axis=1)


def reverse_rows(value):
    return dot(reversal(value.shape[0]), value).astype(value.dtype)


def reverse_both(value):
    return reverse_lanes(reverse_rows(value))


def call(kernel, out_shapes, *operands, scalars=0, scratch=(), flops=0, moved=0):
    specs = [pl.BlockSpec(memory_space=pltpu.SMEM)] * scalars
    specs += [pl.BlockSpec(memory_space=pltpu.VMEM)] * (len(operands) - scalars)
    return pl.pallas_call(
        kernel,
        out_shape=out_shapes,
        in_specs=specs,
        out_specs=[pl.BlockSpec(memory_space=pltpu.VMEM)] * len(out_shapes),
        scratch_shapes=list(scratch),
        cost_estimate=pl.CostEstimate(flops=flops, bytes_accessed=moved, transcendentals=0),
        compiler_params=pltpu.CompilerParams(vmem_limit_bytes=48 * 1024 * 1024),
    )(*operands)


def token_row(ids_ref, mask_ref, strand):
    return jnp.where(mask_ref[strand] == 1, 5, ids_ref[strand]).astype(F32)


def lead_kernel(
    normed_ref, grad_ref, ids_ref, mask_ref, send_ref, tails_ref, heads_ref, far_ref, tokens_ref,
    head, ids, mask, arrived,
):
    rows, width = send_ref.shape
    copies = [
        pltpu.make_async_copy(source, target, arrived.at[place])
        for place, (source, target) in enumerate(
            (
                (normed_ref.at[1], send_ref),
                (normed_ref.at[:, rows - HALO : rows, :], tails_ref),
                (grad_ref.at[:, 0:HALO, :], head),
                (grad_ref.at[1], far_ref),
                (ids_ref, ids),
                (mask_ref, mask),
            )
        )
    ]
    for copy in copies:
        copy.start()
    for copy in copies:
        copy.wait()
    at_row = lax.broadcasted_iota(jnp.int32, (HALO, width), 0) == HALO - 1
    for strand in range(2):
        tokens = token_row(ids, mask, strand)
        tokens_ref[strand] = tokens
        tokens = jnp.concatenate([tokens, jnp.zeros((1, width - LANES), F32)], axis=1)
        heads_ref[strand] = jnp.where(at_row, tokens, head[strand].astype(F32)).astype(BF16)


def spans_of(chunk, width):
    part = width // 4
    starts = (0, 3 * part) if chunk == 0 else (part, 2 * part)
    return [
        (slice(start, start + part), slice(place * part, (place + 1) * part))
        for place, start in enumerate(starts)
    ]


def flip_kernel(grad_ref, *out_refs):
    whole = reverse_both(grad_ref[...])
    for chunk, out_ref in enumerate(out_refs):
        for cols, own in spans_of(chunk, whole.shape[1]):
            out_ref[:, own] = whole[:, cols]


def edge_kernel(tokens_ref, tails_ref, heads_ref, slab_ref):
    width = slab_ref.shape[1]
    head = heads_ref[1].astype(F32)
    swap = reversal(HALO, F32)
    tail_rev = jnp.dot(swap, tails_ref[1].astype(F32), preferred_element_type=F32).astype(BF16)
    head_rev = jnp.dot(swap, head, preferred_element_type=F32).astype(BF16)
    own = tokens_ref[1]
    both = jnp.concatenate([own, head[HALO - 1 : HALO, :LANES], jnp.zeros((6, LANES), F32)], axis=0)
    flipped = dot(both.astype(BF16), reversal(LANES))
    tokens = jnp.concatenate([flipped[0:1], flipped[1:2], jnp.zeros((1, width - 2 * LANES), F32)], axis=1)
    at_row = lax.broadcasted_iota(jnp.int32, (HALO, width), 0) == HALO - 1
    slab_ref[0:HALO, :] = reverse_lanes(head_rev)
    slab_ref[HALO:, :] = jnp.where(at_row, tokens, reverse_lanes(tail_rev).astype(F32)).astype(BF16)


def forward_kernel(
    place_ref, own_ref, near_ref, other_ref, normed_ref, tails_ref, filter_ref, bias_ref,
    weight_ref, values_ref, filter_rev_ref, bias_out_ref, bias_rev_ref,
):
    shard = own_ref.shape[0]
    half = 4 * shard
    x_lo = place_ref[0] // 2
    core = place_ref[0] % 2
    pieces = (
        (own_ref[...], x_lo, core),
        (near_ref[...], 1 - x_lo, core),
        (other_ref[0:shard, :], x_lo, 1 - core),
        (other_ref[shard:, :], 1 - x_lo, 1 - core),
    )
    for block, chip, at_core in pieces:
        index = chip * 2 + at_core
        weight_ref[pl.ds(pl.multiple_of(index * shard, shard), shard), :] = block
        back = half + (3 - index) * shard
        weight_ref[pl.ds(pl.multiple_of(back, shard), shard), :] = reverse_both(block)
    width = weight_ref.shape[1]
    table = jnp.concatenate([bias_ref[...], jnp.zeros((HALO - bias_ref.shape[0], width), F32)], axis=0)
    bias_out_ref[...] = table
    bias_rev_ref[...] = reverse_lanes(table, HIGHEST)
    taps = filter_ref.shape[0]
    table = jnp.concatenate([filter_ref[...], jnp.zeros((HALO - taps, width), F32)], axis=0)
    filter_rev_ref[...] = reverse_lanes(table, HIGHEST)
    weight = weight_ref[...]
    values_ref[HALO:, :] = dot(normed_ref[0], weight).astype(BF16).astype(F32)
    values_ref[0:HALO, :] = dot(tails_ref[0], weight).astype(BF16).astype(F32)


def join_kernel(first_ref, second_ref, out_ref):
    shard = first_ref.shape[0]
    out_ref[0:shard, :] = first_ref[...]
    out_ref[shard:, :] = second_ref[...]


def one_hot(row, count):
    classes = lax.broadcasted_iota(jnp.int32, (HALO, count), 0)
    return (row.astype(jnp.int32) == classes).astype(F32)


def rows_of(hot, table):
    return lax.dot_general(
        hot, table, (((0,), (0,)), ((), ())), preferred_element_type=F32, precision=HIGHEST
    )


def near_strand_kernel(
    count, *refs,
):
    arrived = refs[0][...]
    for ref in refs[1:count]:
        arrived = arrived + ref[...]
    near_strand(arrived, *refs[count:])


def near_strand(
    far, weight_ref, values0_ref, grad_ref, tokens_ref, filter_ref, bias_ref,
    values1_ref, conv_grad_ref, mirror_ref, terms_ref,
):
    rows, width = grad_ref.shape[1], grad_ref.shape[2]
    taps = filter_ref.shape[0]
    values1_ref[...] = dot(reverse_both(far), weight_ref[...]).astype(BF16).astype(F32)
    hot = one_hot(tokens_ref[0], LANES)
    wide = 2 * LANES
    for index in range(width // wide):
        cols = slice(index * wide, (index + 1) * wide)
        weights = filter_ref[:, cols]
        own = grad_ref[0, :, cols].astype(F32)
        gate = jax.nn.sigmoid(values1_ref[:, cols] + rows_of(hot, bias_ref[:, cols]))
        conv_grad = own * gate
        conv_grad_ref[:, cols] = conv_grad
        conv = jnp.zeros((rows, wide), F32)
        for tap in range(taps):
            shifted = values0_ref[HALO - tap : HALO - tap + rows, cols]
            conv = conv + weights[tap : tap + 1] * shifted
            terms_ref[tap : tap + 1, cols] = jnp.sum(conv_grad * shifted, axis=0, keepdims=True)
        pre = own * conv * gate * (1.0 - gate)
        mirror_ref[:, cols] = pre.astype(BF16)
        terms_ref[8:16, cols] = jnp.dot(hot, pre, preferred_element_type=F32, precision=HIGHEST)
    terms_ref[7:8, :] = jnp.zeros((1, width), F32)


def far_strand_kernel(
    chunk, taps, slab_ref, halo_ref, weight_ref, values0_ref, values1_ref, mirror_ref, heads_ref,
    filter_rev_ref, bias_ref, bias_rev_ref,
    send_ref, mirror_out_ref, edge_ref,
    wide1, pull1, sums,
):
    rows, width = mirror_ref.shape
    tokens = halo_ref[HALO:, :].astype(F32)[HALO - 1 : HALO, :]
    hot_own = one_hot(tokens[:, :LANES], LANES)
    hot_far = one_hot(tokens[:, LANES : 2 * LANES], LANES)
    hot_edge = one_hot(heads_ref[0].astype(F32)[HALO - 1 : HALO, :LANES], LANES)
    sums[...] = jnp.zeros_like(sums)
    for cols, local in spans_of(chunk, width):
        edge = dot(halo_ref[HALO:, :], weight_ref[:, cols]).astype(BF16).astype(F32)
        edge_gate = jax.nn.sigmoid(edge + rows_of(hot_edge, bias_ref[:, cols])[0:HALO])
        edge_ref[:, local] = heads_ref[0, :, cols].astype(F32) * edge_gate
        weights = filter_rev_ref[:, cols]
        wide1[0:rows, :] = values1_ref[:, cols]
        wide1[rows:, :] = edge
        own = slab_ref[:, local].astype(F32)
        gate = jax.nn.sigmoid(values0_ref[HALO:, cols] + rows_of(hot_own, bias_rev_ref[:, cols]))
        far_gate = jax.nn.sigmoid(
            values0_ref[0:HALO, cols] + rows_of(hot_far, bias_rev_ref[:, cols])[LANES - HALO :]
        )
        conv_grad = own * gate
        pull1[HALO:, :] = conv_grad
        pull1[0:HALO, :] = halo_ref[0:HALO, cols].astype(F32) * far_gate
        conv = jnp.zeros_like(own)
        for tap in range(taps):
            shifted = wide1[tap : tap + rows, :]
            conv = conv + weights[tap : tap + 1] * shifted
            sums[tap : tap + 1, local] = jnp.sum(conv_grad * shifted, axis=0, keepdims=True)
        pre = own * conv * gate * (1.0 - gate)
        mirror_out_ref[:, local] = pre.astype(BF16)
        sums[8:16, local] = jnp.dot(hot_own, pre, preferred_element_type=F32, precision=HIGHEST)
        total = mirror_ref[:, cols].astype(F32)
        for tap in range(taps):
            total = total + weights[tap : tap + 1] * pull1[HALO - tap : HALO - tap + rows, :]
        send_ref[0:rows, local] = total.astype(BF16)
    send_ref[rows:, :] = sums[...].astype(BF16)


def left_kernel(normed_ref, left_ref):
    rows = normed_ref.shape[1]
    half = normed_ref.shape[2] // 2
    for strand in range(2):
        value = normed_ref[strand]
        left_ref[strand * rows : (strand + 1) * rows, :] = value[:, :half]
        left_ref[(2 + strand) * rows : (3 + strand) * rows, :] = reverse_both(value)[:, :half]


def near_grad_kernel(chunk, conv_grad_ref, edge_ref, mirror_ref, filter_ref, right_ref, pull0):
    rows, width = conv_grad_ref.shape
    for cols, local in spans_of(chunk, width):
        pull0[0:rows, :] = conv_grad_ref[:, cols]
        pull0[rows:, :] = edge_ref[:, local]
        total = mirror_ref[:, local].astype(F32)
        for tap in range(filter_ref.shape[0]):
            total = total + filter_ref[tap : tap + 1, cols] * pull0[tap : tap + rows, :]
        right_ref[0:rows, local] = total.astype(BF16)
    right_ref[rows:, :] = reverse_both(right_ref[0:rows, :])


def project_kernel(
    scale, place_ref, left_ref, right0_ref, right1_ref, back0_ref, back1_ref, terms_ref,
    send_ref, keep_ref, sums_ref, final_ref,
):
    width = terms_ref.shape[1]
    rows = right0_ref.shape[0] // 2
    core = place_ref[0] % 2
    shard = left_ref.shape[1] // 4
    for chunk, (right_ref, back_ref) in enumerate(((right0_ref, back0_ref), (right1_ref, back1_ref))):
        back = back_ref[0:rows, :]
        home = reverse_both(back)
        right = jnp.concatenate([right_ref[0:rows, :], home, right_ref[rows:, :], back], axis=0)
        back_terms = reverse_lanes(back_ref[rows:, :]).astype(F32)
        for cols, local in spans_of(chunk, width):
            final_ref[0, :, cols] = right_ref[0:rows, local]
            final_ref[1, :, cols] = home[:, local]
            sums = (terms_ref[:, cols] + back_terms[:, local]) * scale
            sums_ref[:, cols] = sums
            send_ref[2 * shard :, cols] = sums.astype(BF16)
        for chip in range(2):
            for mine in range(2):
                index = chip * 2 + (core if mine else 1 - core)
                left = left_ref[:, pl.ds(pl.multiple_of(index * shard, shard), shard)]
                part = lax.dot_general(left, right, (((0,), (0,)), ((), ())), preferred_element_type=F32) * scale
                place = slice(chip * shard, (chip + 1) * shard)
                for cols, local in spans_of(chunk, width):
                    if mine:
                        keep_ref[place, cols] = part[:, local]
                    else:
                        send_ref[place, cols] = part[:, local].astype(BF16)


def input_grad_kernel(value_grad_ref, weight_ref, out_ref):
    weight = weight_ref[...]
    for strand in range(2):
        out_ref[strand] = lax.dot_general(
            value_grad_ref[strand], weight, (((1,), (1,)), ((), ())), preferred_element_type=F32
        ).astype(BF16)


def first_sum_kernel(place_ref, keep_ref, got_ref, sums_ref, send_ref, keep_out_ref, sums_out_ref):
    shard = keep_ref.shape[0] // 2
    x_lo = place_ref[0] // 2
    here = pl.ds(pl.multiple_of(x_lo * shard, shard), shard)
    there = pl.ds(pl.multiple_of((1 - x_lo) * shard, shard), shard)
    keep_out_ref[...] = keep_ref[here, :] + got_ref[here, :].astype(F32)
    send_ref[0:shard, :] = (keep_ref[there, :] + got_ref[there, :].astype(F32)).astype(BF16)
    sums = sums_ref[...] + got_ref[2 * shard :, :].astype(F32)
    sums_out_ref[...] = sums
    send_ref[shard:, :] = sums.astype(BF16)


def last_sum_kernel(place_ref, keep_ref, got_ref, sums_ref, proj_ref, filter_ref, bias_ref):
    shard = keep_ref.shape[0]
    part = filter_ref.shape[2]
    proj_ref[...] = keep_ref[...] + got_ref[0:shard, :].astype(F32)
    cols = pl.ds(pl.multiple_of(place_ref[0] * part, part), part)
    sums = sums_ref[:, cols] + got_ref[shard:, cols].astype(F32)
    for tap in range(filter_ref.shape[0]):
        filter_ref[tap] = sums[tap : tap + 1, :]
    for token in range(bias_ref.shape[0]):
        bias_ref[token] = sums[8 + token : 9 + token, :]


def mirror_groups(size):
    planes = max(size // PLANE, 1)
    groups = ([], [])
    for index in range(size):
        apart = abs(planes - 1 - 2 * (index // PLANE))
        groups[min(apart, planes - apart) > 3].append(index)
    return groups


def mirrored(value, sources=None):
    size = lax.axis_size("ctx")
    return lax.ppermute(value, "ctx", [(i, size - 1 - i) for i in sources or range(size)])


def shifted(value, distance):
    devices = range(lax.axis_size("ctx"))
    return lax.ppermute(value, "ctx", [(i, i + distance) for i in devices if i + distance in devices])


def partner(value, bit):
    return lax.ppermute(value, "fsdp", [(i, i ^ bit) for i in range(lax.axis_size("fsdp"))])


def shape(dims, dtype):
    return jax.ShapeDtypeStruct(dims, dtype)


def step(normed, out_grad, ids, mask, proj_half, conv_filter, gate_bias):
    rows, width = normed.shape[2], normed.shape[3]
    taps = conv_filter.shape[0]
    shard = proj_half.shape[0]
    classes = gate_bias.shape[0]
    normed, out_grad = normed[:, 0], out_grad[:, 0]
    place = lax.axis_index("fsdp").astype(jnp.int32).reshape(1)

    send, tails, heads, far_grad, tokens = pl.pallas_call(
        lead_kernel,
        out_shape=(
            shape((rows, width), BF16),
            shape((2, HALO, width), BF16),
            shape((2, HALO, width), BF16),
            shape((rows, width), BF16),
            shape((2, 1, rows), F32),
        ),
        in_specs=[pl.BlockSpec(memory_space=pltpu.HBM)] * 4,
        out_specs=[pl.BlockSpec(memory_space=pltpu.VMEM)] * 5,
        scratch_shapes=[
            pltpu.VMEM((2, HALO, width), BF16),
            pltpu.VMEM((2, 1, rows), jnp.int32),
            pltpu.VMEM((2, 1, rows), jnp.int32),
            pltpu.SemaphoreType.DMA((6,)),
        ],
        cost_estimate=pl.CostEstimate(flops=0, bytes_accessed=4 * rows * width, transcendentals=0),
    )(normed, out_grad, ids, mask)
    first, second = mirror_groups(lax.axis_size("ctx"))
    arrivals = [mirrored(send, first)]
    if second:
        arrivals.append(mirrored(send, second))
    heads = shifted(heads, -1)
    tails = shifted(tails, 1)
    half = width // 2
    far_grads = call(
        flip_kernel, (shape((rows, half), BF16),) * 2, far_grad, flops=600 * rows * width, moved=4 * rows * width,
    )
    slabs = [mirrored(far) for far in far_grads]
    near = partner(proj_half, 2)
    halo, = call(
        edge_kernel, (shape((2 * HALO, width), BF16),), tokens, tails, heads,
        flops=600 * HALO * width, moved=8 * HALO * width,
    )
    halo = mirrored(halo)
    pair, = call(join_kernel, (shape((2 * shard, width), BF16),), proj_half, near, moved=8 * shard * width)
    other = partner(pair, 1)
    weight, values0, filter_rev, bias, bias_rev = call(
        forward_kernel,
        (shape((width, width), BF16), shape((rows + HALO, width), F32)) + (shape((HALO, width), F32),) * 3,
        place, proj_half, near, other, normed, tails, conv_filter, gate_bias, scalars=1,
        flops=2 * rows * width * width, moved=6 * width * width,
    )
    values1, conv_grad, mirror0, terms = call(
        functools.partial(near_strand_kernel, len(arrivals)),
        (
            shape((rows, width), F32),
            shape((rows, width), F32),
            shape((rows, width), BF16),
            shape((16, width), F32),
        ),
        *arrivals, weight, values0, out_grad, tokens, conv_filter, bias,
        flops=2 * rows * width * width, moved=8 * width * width,
    )
    left, = call(left_kernel, (shape((4 * rows, half), BF16),), normed, flops=rows * width * width)
    grad_scale = 1.0 / math.sqrt(2.0 * lax.axis_size("fsdp") * rows)
    part = width // lax.axis_size("fsdp")
    chunks = []
    for chunk in range(2):
        window = pltpu.VMEM((rows + HALO, part), F32)
        send, mirror1, edge = call(
            functools.partial(far_strand_kernel, chunk, taps),
            (shape((rows + 16, half), BF16), shape((rows, half), BF16), shape((HALO, half), F32)),
            slabs[chunk], halo, weight, values0, values1, mirror0, heads, filter_rev, bias, bias_rev,
            scratch=[window, window, pltpu.VMEM((16, half), F32)],
            flops=rows * width * width, moved=4 * width * width,
        )
        back = mirrored(send)
        right, = call(
            functools.partial(near_grad_kernel, chunk), (shape((2 * rows, half), BF16),),
            conv_grad, edge, mirror1, conv_filter,
            scratch=[window], flops=rows * width * width // 2, moved=8 * rows * width,
        )
        chunks.append((back, right))
    (back0, right0), (back1, right1) = chunks
    send1, keep1, sums1, final = call(
        functools.partial(project_kernel, grad_scale),
        (
            shape((2 * shard + 16, width), BF16),
            shape((2 * shard, width), F32),
            shape((16, width), F32),
            shape((2, rows, width), BF16),
        ),
        place, left, right0, right1, back0, back1, terms, scalars=1,
        flops=4 * rows * width * width, moved=4 * width * width,
    )
    got1 = partner(send1, 1)
    send2, keep2, sums2 = call(
        first_sum_kernel,
        (shape((shard + 16, width), BF16), shape((shard, width), F32), shape((16, width), F32)),
        place, keep1, got1, sums1, scalars=1, moved=16 * shard * width,
    )
    got2 = partner(send2, 2)
    in_grad, = call(
        input_grad_kernel, (shape((2, rows, width), BF16),), final, weight,
        flops=4 * rows * width * width, moved=4 * width * width,
    )
    proj_grad, filter_grad, bias_grad = call(
        last_sum_kernel,
        (shape((shard, width), F32), shape((taps, 1, part), F32), shape((classes, 1, part), F32)),
        place, keep2, got2, sums2, scalars=1, moved=12 * shard * width,
    )
    return (
        in_grad[:, None],
        proj_grad[None],
        jnp.transpose(filter_grad, (1, 0, 2)),
        jnp.transpose(bias_grad, (1, 0, 2)),
    )


def solution(mesh):
    placed = (
        P(None, "fsdp", "ctx", None),
        P(None, "fsdp", "ctx", None),
        P(None, "fsdp", "ctx"),
        P(None, "fsdp", "ctx"),
        P("fsdp", None),
        P(),
        P(),
    )
    return jax.shard_map(
        step,
        mesh=mesh,
        in_specs=placed,
        out_specs=(
            P(None, "fsdp", "ctx", None),
            P("ctx", "fsdp", None),
            P("ctx", None, "fsdp"),
            P("ctx", None, "fsdp"),
        ),
        check_vma=False,
    )
```

```python
import functools
import math

import jax
import jax.numpy as jnp
from jax import lax
from jax.experimental import pallas as pl
from jax.experimental.pallas import tpu as pltpu
from jax.sharding import PartitionSpec as P


LANES = 128
HALO = 8
VMEM_BYTES = 20 * 1024 * 1024
F32 = jnp.float32
BF16 = jnp.bfloat16
HIGHEST = lax.Precision.HIGHEST


def dot(a, b):
    return jnp.dot(a, b, preferred_element_type=F32)


def reversal(size, dtype=BF16):
    rows = lax.broadcasted_iota(jnp.int32, (size, size), 0)
    cols = lax.broadcasted_iota(jnp.int32, (size, size), 1)
    return (rows + cols == size - 1).astype(dtype)


def reverse_lanes(value, precision=None):
    count = value.shape[-1] // LANES
    swap = reversal(LANES, value.dtype)
    parts = []
    for block in reversed(range(count)):
        part = value[:, block * LANES : (block + 1) * LANES]
        parts.append(
            jnp.dot(part, swap, preferred_element_type=F32, precision=precision).astype(value.dtype)
        )
    return jnp.concatenate(parts, axis=1)


def reverse_rows(value):
    return dot(reversal(value.shape[0]), value).astype(value.dtype)


def reverse_both(value):
    return reverse_lanes(reverse_rows(value))


def call(kernel, out_shapes, *operands, scalars=0, scratch=(), flops=0, moved=0):
    specs = [pl.BlockSpec(memory_space=pltpu.SMEM)] * scalars
    specs += [pl.BlockSpec(memory_space=pltpu.VMEM)] * (len(operands) - scalars)
    return pl.pallas_call(
        kernel,
        out_shape=out_shapes,
        in_specs=specs,
        out_specs=[pl.BlockSpec(memory_space=pltpu.VMEM)] * len(out_shapes),
        scratch_shapes=list(scratch),
        cost_estimate=pl.CostEstimate(flops=flops, bytes_accessed=moved, transcendentals=0),
        compiler_params=pltpu.CompilerParams(vmem_limit_bytes=VMEM_BYTES),
    )(*operands)


def token_row(ids_ref, mask_ref, strand):
    return jnp.where(mask_ref[strand] == 1, 5, ids_ref[strand]).astype(F32)


def lead_kernel(
    normed_ref, grad_ref, ids_ref, mask_ref, send_ref, tails_ref, heads_ref, far_ref, tokens_ref,
    head, ids, mask, arrived,
):
    rows, width = send_ref.shape
    copies = [
        pltpu.make_async_copy(source, target, arrived.at[place])
        for place, (source, target) in enumerate(
            (
                (normed_ref.at[1], send_ref),
                (normed_ref.at[:, rows - HALO : rows, :], tails_ref),
                (grad_ref.at[:, 0:HALO, :], head),
                (grad_ref.at[1], far_ref),
                (ids_ref, ids),
                (mask_ref, mask),
            )
        )
    ]
    for copy in copies:
        copy.start()
    for copy in copies:
        copy.wait()
    at_row = lax.broadcasted_iota(jnp.int32, (HALO, width), 0) == HALO - 1
    for strand in range(2):
        tokens = token_row(ids, mask, strand)
        tokens_ref[strand] = tokens
        tokens = jnp.concatenate([tokens, jnp.zeros((1, width - LANES), F32)], axis=1)
        heads_ref[strand] = jnp.where(at_row, tokens, head[strand].astype(F32)).astype(BF16)


def pack_kernel(grad_ref, tokens_ref, tails_ref, heads_ref, slab_ref):
    rows, width = grad_ref.shape
    head = heads_ref[1].astype(F32)
    swap = reversal(HALO, F32)
    tail_rev = jnp.dot(swap, tails_ref[1].astype(F32), preferred_element_type=F32).astype(BF16)
    head_rev = jnp.dot(swap, head, preferred_element_type=F32).astype(BF16)
    own = tokens_ref[1]
    both = jnp.concatenate([own, head[HALO - 1 : HALO, :LANES], jnp.zeros((6, LANES), F32)], axis=0)
    flipped = dot(both.astype(BF16), reversal(LANES))
    tokens = jnp.concatenate([flipped[0:1], flipped[1:2], jnp.zeros((1, width - 2 * LANES), F32)], axis=1)
    at_row = lax.broadcasted_iota(jnp.int32, (HALO, width), 0) == HALO - 1
    slab_ref[0:HALO, :] = reverse_lanes(head_rev)
    slab_ref[HALO : HALO + rows, :] = reverse_both(grad_ref[...])
    slab_ref[HALO + rows :, :] = jnp.where(at_row, tokens, reverse_lanes(tail_rev).astype(F32)).astype(BF16)


def forward_kernel(
    place_ref, own_ref, near_ref, other_ref, normed_ref, tails_ref, filter_ref, bias_ref,
    weight_ref, values_ref, filter_rev_ref, bias_out_ref, bias_rev_ref,
):
    shard = own_ref.shape[0]
    half = 4 * shard
    x_lo = place_ref[0] // 2
    core = place_ref[0] % 2
    pieces = (
        (own_ref[...], x_lo, core),
        (near_ref[...], 1 - x_lo, core),
        (other_ref[0:shard, :], x_lo, 1 - core),
        (other_ref[shard:, :], 1 - x_lo, 1 - core),
    )
    for block, chip, at_core in pieces:
        index = chip * 2 + at_core
        weight_ref[pl.ds(pl.multiple_of(index * shard, shard), shard), :] = block
        back = half + (3 - index) * shard
        weight_ref[pl.ds(pl.multiple_of(back, shard), shard), :] = reverse_both(block)
    width = weight_ref.shape[1]
    table = jnp.concatenate([bias_ref[...], jnp.zeros((HALO - bias_ref.shape[0], width), F32)], axis=0)
    bias_out_ref[...] = table
    bias_rev_ref[...] = reverse_lanes(table, HIGHEST)
    taps = filter_ref.shape[0]
    table = jnp.concatenate([filter_ref[...], jnp.zeros((HALO - taps, width), F32)], axis=0)
    filter_rev_ref[...] = reverse_lanes(table, HIGHEST)
    weight = weight_ref[...]
    values_ref[HALO:, :] = dot(normed_ref[0], weight).astype(BF16).astype(F32)
    values_ref[0:HALO, :] = dot(tails_ref[0], weight).astype(BF16).astype(F32)


def join_kernel(first_ref, second_ref, out_ref):
    shard = first_ref.shape[0]
    out_ref[0:shard, :] = first_ref[...]
    out_ref[shard:, :] = second_ref[...]


def one_hot(row, count):
    classes = lax.broadcasted_iota(jnp.int32, (HALO, count), 0)
    return (row.astype(jnp.int32) == classes).astype(F32)


def rows_of(hot, table):
    return lax.dot_general(
        hot, table, (((0,), (0,)), ((), ())), preferred_element_type=F32, precision=HIGHEST
    )


def near_strand_kernel(
    far_ref, weight_ref, values0_ref, grad_ref, tokens_ref, filter_ref, bias_ref,
    values1_ref, conv_grad_ref, mirror_ref, terms_ref,
):
    rows, width = grad_ref.shape[1], grad_ref.shape[2]
    taps = filter_ref.shape[0]
    values1_ref[...] = dot(reverse_both(far_ref[...]), weight_ref[...]).astype(BF16).astype(F32)
    hot = one_hot(tokens_ref[0], LANES)
    wide = 2 * LANES
    for index in range(width // wide):
        cols = slice(index * wide, (index + 1) * wide)
        weights = filter_ref[:, cols]
        own = grad_ref[0, :, cols].astype(F32)
        gate = jax.nn.sigmoid(values1_ref[:, cols] + rows_of(hot, bias_ref[:, cols]))
        conv_grad = own * gate
        conv_grad_ref[:, cols] = conv_grad
        conv = jnp.zeros((rows, wide), F32)
        for tap in range(taps):
            shifted = values0_ref[HALO - tap : HALO - tap + rows, cols]
            conv = conv + weights[tap : tap + 1] * shifted
            terms_ref[tap : tap + 1, cols] = jnp.sum(conv_grad * shifted, axis=0, keepdims=True)
        pre = own * conv * gate * (1.0 - gate)
        mirror_ref[:, cols] = pre.astype(BF16)
        terms_ref[8:16, cols] = jnp.dot(hot, pre, preferred_element_type=F32, precision=HIGHEST)
    terms_ref[7:8, :] = jnp.zeros((1, width), F32)


def far_strand_kernel(
    taps, slab_ref, weight_ref, values0_ref, values1_ref, mirror_ref, heads_ref,
    filter_rev_ref, bias_ref, bias_rev_ref,
    send_ref, mirror_out_ref, edge_ref,
    wide1, pull1, sums,
):
    rows, width = mirror_ref.shape
    tokens = slab_ref[HALO + rows :, :].astype(F32)[HALO - 1 : HALO, :]
    hot_own = one_hot(tokens[:, :LANES], LANES)
    hot_far = one_hot(tokens[:, LANES : 2 * LANES], LANES)
    hot_edge = one_hot(heads_ref[0].astype(F32)[HALO - 1 : HALO, :LANES], LANES)
    edge = dot(slab_ref[HALO + rows :, :], weight_ref[...]).astype(BF16).astype(F32)
    edge_gate = jax.nn.sigmoid(edge + rows_of(hot_edge, bias_ref[...])[0:HALO])
    edge_ref[...] = heads_ref[0].astype(F32) * edge_gate
    sums[...] = jnp.zeros_like(sums)
    wide = 2 * LANES
    for index in range(width // wide):
        cols = slice(index * wide, (index + 1) * wide)
        weights = filter_rev_ref[:, cols]
        wide1[0:rows, :] = values1_ref[:, cols]
        wide1[rows:, :] = edge[:, cols]
        own = slab_ref[HALO : HALO + rows, cols].astype(F32)
        gate = jax.nn.sigmoid(values0_ref[HALO:, cols] + rows_of(hot_own, bias_rev_ref[:, cols]))
        far_gate = jax.nn.sigmoid(
            values0_ref[0:HALO, cols] + rows_of(hot_far, bias_rev_ref[:, cols])[LANES - HALO :]
        )
        conv_grad = own * gate
        pull1[HALO:, :] = conv_grad
        pull1[0:HALO, :] = slab_ref[0:HALO, cols].astype(F32) * far_gate
        conv = jnp.zeros((rows, wide), F32)
        for tap in range(taps):
            shifted = wide1[tap : tap + rows, :]
            conv = conv + weights[tap : tap + 1] * shifted
            sums[tap : tap + 1, cols] = jnp.sum(conv_grad * shifted, axis=0, keepdims=True)
        pre = own * conv * gate * (1.0 - gate)
        mirror_out_ref[:, cols] = pre.astype(BF16)
        sums[8:16, cols] = jnp.dot(hot_own, pre, preferred_element_type=F32, precision=HIGHEST)
        total = mirror_ref[:, cols].astype(F32)
        for tap in range(taps):
            total = total + weights[tap : tap + 1] * pull1[HALO - tap : HALO - tap + rows, :]
        send_ref[0:rows, cols] = total.astype(BF16)
    send_ref[rows:, :] = sums[...].astype(BF16)


def operands_kernel(
    normed_ref, conv_grad_ref, edge_ref, mirror_ref, filter_ref, left_ref, right_ref, pull0,
):
    rows, width = conv_grad_ref.shape
    half = width // 2
    pull0[0:rows, :] = conv_grad_ref[...]
    pull0[rows:, :] = edge_ref[...]
    for strand in range(2):
        value = normed_ref[strand]
        left_ref[strand * rows : (strand + 1) * rows, :] = value[:, :half]
        left_ref[(2 + strand) * rows : (3 + strand) * rows, :] = reverse_both(value)[:, :half]
    wide = 2 * LANES
    for index in range(width // wide):
        cols = slice(index * wide, (index + 1) * wide)
        total = mirror_ref[:, cols].astype(F32)
        for tap in range(filter_ref.shape[0]):
            total = total + filter_ref[tap : tap + 1, cols] * pull0[tap : tap + rows, cols]
        right_ref[0:rows, cols] = total.astype(BF16)
    right_ref[rows:, :] = reverse_both(right_ref[0:rows, :])


def project_kernel(
    place_ref, scale, left_ref, right_ref, back_ref, terms_ref,
    send_ref, keep_ref, sums_ref, final_ref,
):
    rows = right_ref.shape[0] // 2
    back = back_ref[0:rows, :]
    home = reverse_both(back)
    final_ref[0] = right_ref[0:rows, :]
    final_ref[1] = home
    right = jnp.concatenate([right_ref[0:rows, :], home, right_ref[rows:, :], back], axis=0)
    sums = (terms_ref[...] + reverse_lanes(back_ref[rows:, :]).astype(F32)) * scale
    sums_ref[...] = sums
    core = place_ref[0] % 2
    shard = left_ref.shape[1] // 4
    for chip in range(2):
        for mine in range(2):
            index = chip * 2 + (core if mine else 1 - core)
            left = left_ref[:, pl.ds(pl.multiple_of(index * shard, shard), shard)]
            part = lax.dot_general(left, right, (((0,), (0,)), ((), ())), preferred_element_type=F32) * scale
            if mine:
                keep_ref[chip * shard : (chip + 1) * shard, :] = part
            else:
                send_ref[chip * shard : (chip + 1) * shard, :] = part.astype(BF16)
    send_ref[2 * shard :, :] = sums.astype(BF16)


def input_grad_kernel(value_grad_ref, weight_ref, out_ref):
    weight = weight_ref[...]
    for strand in range(2):
        out_ref[strand] = lax.dot_general(
            value_grad_ref[strand], weight, (((1,), (1,)), ((), ())), preferred_element_type=F32
        ).astype(BF16)


def first_sum_kernel(place_ref, keep_ref, got_ref, sums_ref, send_ref, keep_out_ref, sums_out_ref):
    shard = keep_ref.shape[0] // 2
    x_lo = place_ref[0] // 2
    here = pl.ds(pl.multiple_of(x_lo * shard, shard), shard)
    there = pl.ds(pl.multiple_of((1 - x_lo) * shard, shard), shard)
    keep_out_ref[...] = keep_ref[here, :] + got_ref[here, :].astype(F32)
    send_ref[0:shard, :] = (keep_ref[there, :] + got_ref[there, :].astype(F32)).astype(BF16)
    sums = sums_ref[...] + got_ref[2 * shard :, :].astype(F32)
    sums_out_ref[...] = sums
    send_ref[shard:, :] = sums.astype(BF16)


def last_sum_kernel(place_ref, keep_ref, got_ref, sums_ref, proj_ref, filter_ref, bias_ref):
    shard = keep_ref.shape[0]
    part = filter_ref.shape[2]
    proj_ref[...] = keep_ref[...] + got_ref[0:shard, :].astype(F32)
    cols = pl.ds(pl.multiple_of(place_ref[0] * part, part), part)
    sums = sums_ref[:, cols] + got_ref[shard:, cols].astype(F32)
    for tap in range(filter_ref.shape[0]):
        filter_ref[tap] = sums[tap : tap + 1, :]
    for token in range(bias_ref.shape[0]):
        bias_ref[token] = sums[8 + token : 9 + token, :]


def mirrored(value):
    size = lax.axis_size("ctx")
    return lax.ppermute(value, "ctx", [(i, size - 1 - i) for i in range(size)])


def shifted(value, distance):
    devices = range(lax.axis_size("ctx"))
    return lax.ppermute(value, "ctx", [(i, i + distance) for i in devices if i + distance in devices])


def partner(value, bit):
    return lax.ppermute(value, "fsdp", [(i, i ^ bit) for i in range(lax.axis_size("fsdp"))])


def shape(dims, dtype):
    return jax.ShapeDtypeStruct(dims, dtype)


def step(normed, out_grad, ids, mask, proj_half, conv_filter, gate_bias):
    rows, width = normed.shape[2], normed.shape[3]
    taps = conv_filter.shape[0]
    shard = proj_half.shape[0]
    classes = gate_bias.shape[0]
    normed, out_grad = normed[:, 0], out_grad[:, 0]
    place = lax.axis_index("fsdp").astype(jnp.int32).reshape(1)

    send, tails, heads, far_grad, tokens = pl.pallas_call(
        lead_kernel,
        out_shape=(
            shape((rows, width), BF16),
            shape((2, HALO, width), BF16),
            shape((2, HALO, width), BF16),
            shape((rows, width), BF16),
            shape((2, 1, rows), F32),
        ),
        in_specs=[pl.BlockSpec(memory_space=pltpu.HBM)] * 4,
        out_specs=[pl.BlockSpec(memory_space=pltpu.VMEM)] * 5,
        scratch_shapes=[
            pltpu.VMEM((2, HALO, width), BF16),
            pltpu.VMEM((2, 1, rows), jnp.int32),
            pltpu.VMEM((2, 1, rows), jnp.int32),
            pltpu.SemaphoreType.DMA((6,)),
        ],
        cost_estimate=pl.CostEstimate(flops=0, bytes_accessed=4 * rows * width, transcendentals=0),
    )(normed, out_grad, ids, mask)
    normed_far = mirrored(send)
    heads = shifted(heads, -1)
    tails = shifted(tails, 1)
    near = partner(proj_half, 2)
    slab, = call(
        pack_kernel, (shape((rows + 2 * HALO, width), BF16),), far_grad, tokens, tails, heads,
        flops=600 * rows * width, moved=4 * rows * width,
    )
    slab = mirrored(slab)
    pair, = call(join_kernel, (shape((2 * shard, width), BF16),), proj_half, near, moved=8 * shard * width)
    other = partner(pair, 1)
    weight, values0, filter_rev, bias, bias_rev = call(
        forward_kernel,
        (shape((width, width), BF16), shape((rows + HALO, width), F32)) + (shape((HALO, width), F32),) * 3,
        place, proj_half, near, other, normed, tails, conv_filter, gate_bias, scalars=1,
        flops=2 * rows * width * width, moved=6 * width * width,
    )
    values1, conv_grad, mirror0, terms = call(
        near_strand_kernel,
        (
            shape((rows, width), F32),
            shape((rows, width), F32),
            shape((rows, width), BF16),
            shape((16, width), F32),
        ),
        normed_far, weight, values0, out_grad, tokens, conv_filter, bias,
        flops=2 * rows * width * width, moved=8 * width * width,
    )
    wide = 2 * LANES
    send, mirror1, edge = call(
        functools.partial(far_strand_kernel, taps),
        (shape((rows + 16, width), BF16), shape((rows, width), BF16), shape((HALO, width), F32)),
        slab, weight, values0, values1, mirror0, heads, filter_rev, bias, bias_rev,
        scratch=[pltpu.VMEM((rows + HALO, wide), F32)] * 2 + [pltpu.VMEM((16, width), F32)],
        flops=2 * rows * width * width, moved=8 * width * width,
    )
    back = mirrored(send)
    left, right = call(
        operands_kernel, (shape((4 * rows, width // 2), BF16), shape((2 * rows, width), BF16)),
        normed, conv_grad, edge, mirror1, conv_filter,
        scratch=[pltpu.VMEM((rows + HALO, width), F32)],
        flops=rows * width * width, moved=16 * rows * width,
    )
    grad_scale = 1.0 / math.sqrt(2.0 * lax.axis_size("fsdp") * rows)
    send1, keep1, sums1, final = call(
        lambda place_ref, *refs: project_kernel(place_ref, grad_scale, *refs),
        (
            shape((2 * shard + 16, width), BF16),
            shape((2 * shard, width), F32),
            shape((16, width), F32),
            shape((2, rows, width), BF16),
        ),
        place, left, right, back, terms, scalars=1,
        flops=4 * rows * width * width, moved=4 * width * width,
    )
    got1 = partner(send1, 1)
    send2, keep2, sums2 = call(
        first_sum_kernel,
        (shape((shard + 16, width), BF16), shape((shard, width), F32), shape((16, width), F32)),
        place, keep1, got1, sums1, scalars=1, moved=16 * shard * width,
    )
    got2 = partner(send2, 2)
    in_grad, = call(
        input_grad_kernel, (shape((2, rows, width), BF16),), final, weight,
        flops=4 * rows * width * width, moved=4 * width * width,
    )
    part = width // lax.axis_size("fsdp")
    proj_grad, filter_grad, bias_grad = call(
        last_sum_kernel,
        (shape((shard, width), F32), shape((taps, 1, part), F32), shape((classes, 1, part), F32)),
        place, keep2, got2, sums2, scalars=1, moved=12 * shard * width,
    )
    return (
        in_grad[:, None],
        proj_grad[None],
        jnp.transpose(filter_grad, (1, 0, 2)),
        jnp.transpose(bias_grad, (1, 0, 2)),
    )


def solution(mesh):
    placed = (
        P(None, "fsdp", "ctx", None),
        P(None, "fsdp", "ctx", None),
        P(None, "fsdp", "ctx"),
        P(None, "fsdp", "ctx"),
        P("fsdp", None),
        P(),
        P(),
    )
    return jax.shard_map(
        step,
        mesh=mesh,
        in_specs=placed,
        out_specs=(
            P(None, "fsdp", "ctx", None),
            P("ctx", "fsdp", None),
            P("ctx", None, "fsdp"),
            P("ctx", None, "fsdp"),
        ),
        check_vma=False,
    )
```

```python
import functools
import math

import jax
import jax.numpy as jnp
from jax import lax
from jax.experimental import pallas as pl
from jax.experimental.pallas import tpu as pltpu
from jax.sharding import PartitionSpec as P


LANES = 128
HALO = 8
VMEM_BYTES = 20 * 1024 * 1024
F32 = jnp.float32
BF16 = jnp.bfloat16
HIGHEST = lax.Precision.HIGHEST


def dot(a, b):
    return jnp.dot(a, b, preferred_element_type=F32)


def reversal(size, dtype=BF16):
    rows = lax.broadcasted_iota(jnp.int32, (size, size), 0)
    cols = lax.broadcasted_iota(jnp.int32, (size, size), 1)
    return (rows + cols == size - 1).astype(dtype)


def reverse_lanes(value, precision=None):
    count = value.shape[-1] // LANES
    swap = reversal(LANES, value.dtype)
    parts = []
    for block in reversed(range(count)):
        part = value[:, block * LANES : (block + 1) * LANES]
        parts.append(
            jnp.dot(part, swap, preferred_element_type=F32, precision=precision).astype(value.dtype)
        )
    return jnp.concatenate(parts, axis=1)


def reverse_rows(value):
    return dot(reversal(value.shape[0]), value).astype(value.dtype)


def reverse_both(value):
    return reverse_lanes(reverse_rows(value))


def call(kernel, out_shapes, *operands, scalars=0, scratch=(), flops=0, moved=0):
    specs = [pl.BlockSpec(memory_space=pltpu.SMEM)] * scalars
    specs += [pl.BlockSpec(memory_space=pltpu.VMEM)] * (len(operands) - scalars)
    return pl.pallas_call(
        kernel,
        out_shape=out_shapes,
        in_specs=specs,
        out_specs=[pl.BlockSpec(memory_space=pltpu.VMEM)] * len(out_shapes),
        scratch_shapes=list(scratch),
        cost_estimate=pl.CostEstimate(flops=flops, bytes_accessed=moved, transcendentals=0),
        compiler_params=pltpu.CompilerParams(vmem_limit_bytes=VMEM_BYTES),
    )(*operands)


def token_row(ids_ref, mask_ref, strand):
    return jnp.where(mask_ref[strand] == 1, 5, ids_ref[strand]).astype(F32)


def lead_kernel(
    normed_ref, grad_ref, ids_ref, mask_ref, send_ref, tails_ref, heads_ref, far_ref, tokens_ref, rims_ref,
    head, ids, mask, arrived,
):
    rows, width = send_ref.shape
    copies = [
        pltpu.make_async_copy(source, target, arrived.at[place])
        for place, (source, target) in enumerate(
            (
                (normed_ref.at[1], send_ref),
                (normed_ref.at[:, rows - HALO : rows, :], tails_ref),
                (grad_ref.at[:, 0:HALO, :], head),
                (grad_ref.at[1], far_ref),
                (ids_ref, ids),
                (mask_ref, mask),
            )
        )
    ]
    for copy in copies:
        copy.start()
    for copy in copies:
        copy.wait()
    at_row = lax.broadcasted_iota(jnp.int32, (HALO, width), 0) == HALO - 1
    for strand in range(2):
        tokens = token_row(ids, mask, strand)
        tokens_ref[strand] = tokens
        tokens = jnp.concatenate([tokens, jnp.zeros((1, width - LANES), F32)], axis=1)
        head_rows = jnp.where(at_row, tokens, head[strand].astype(F32)).astype(BF16)
        heads_ref[strand] = head_rows
        rims_ref[strand] = tails_ref[strand]
        rims_ref[2 + strand] = head_rows


def pack_kernel(
    middle, shard_ref, grad_ref, tokens_ref, near_tails_ref, near_heads_ref, rims_ref, slab_ref, tails_ref, heads_ref,
):
    rows, width = grad_ref.shape
    for strand in range(2):
        tails_ref[strand] = jnp.where(shard_ref[0] == middle, rims_ref[strand], near_tails_ref[strand])
        heads_ref[strand] = jnp.where(shard_ref[0] == middle - 1, rims_ref[2 + strand], near_heads_ref[strand])
    head = heads_ref[1].astype(F32)
    swap = reversal(HALO, F32)
    tail_rev = jnp.dot(swap, tails_ref[1].astype(F32), preferred_element_type=F32).astype(BF16)
    head_rev = jnp.dot(swap, head, preferred_element_type=F32).astype(BF16)
    own = tokens_ref[1]
    both = jnp.concatenate([own, head[HALO - 1 : HALO, :LANES], jnp.zeros((6, LANES), F32)], axis=0)
    flipped = dot(both.astype(BF16), reversal(LANES))
    tokens = jnp.concatenate([flipped[0:1], flipped[1:2], jnp.zeros((1, width - 2 * LANES), F32)], axis=1)
    at_row = lax.broadcasted_iota(jnp.int32, (HALO, width), 0) == HALO - 1
    slab_ref[0:HALO, :] = reverse_lanes(head_rev)
    slab_ref[HALO : HALO + rows, :] = reverse_both(grad_ref[...])
    slab_ref[HALO + rows :, :] = jnp.where(at_row, tokens, reverse_lanes(tail_rev).astype(F32)).astype(BF16)


def forward_kernel(
    place_ref, own_ref, near_ref, other_ref, normed_ref, tails_ref, filter_ref, bias_ref,
    weight_ref, values_ref, filter_rev_ref, bias_out_ref, bias_rev_ref,
):
    shard = own_ref.shape[0]
    half = 4 * shard
    x_lo = place_ref[0] // 2
    core = place_ref[0] % 2
    pieces = (
        (own_ref[...], x_lo, core),
        (near_ref[...], 1 - x_lo, core),
        (other_ref[0:shard, :], x_lo, 1 - core),
        (other_ref[shard:, :], 1 - x_lo, 1 - core),
    )
    for block, chip, at_core in pieces:
        index = chip * 2 + at_core
        weight_ref[pl.ds(pl.multiple_of(index * shard, shard), shard), :] = block
        back = half + (3 - index) * shard
        weight_ref[pl.ds(pl.multiple_of(back, shard), shard), :] = reverse_both(block)
    width = weight_ref.shape[1]
    table = jnp.concatenate([bias_ref[...], jnp.zeros((HALO - bias_ref.shape[0], width), F32)], axis=0)
    bias_out_ref[...] = table
    bias_rev_ref[...] = reverse_lanes(table, HIGHEST)
    taps = filter_ref.shape[0]
    table = jnp.concatenate([filter_ref[...], jnp.zeros((HALO - taps, width), F32)], axis=0)
    filter_rev_ref[...] = reverse_lanes(table, HIGHEST)
    weight = weight_ref[...]
    values_ref[HALO:, :] = dot(normed_ref[0], weight).astype(BF16).astype(F32)
    values_ref[0:HALO, :] = dot(tails_ref[0], weight).astype(BF16).astype(F32)


def join_kernel(first_ref, second_ref, out_ref):
    shard = first_ref.shape[0]
    out_ref[0:shard, :] = first_ref[...]
    out_ref[shard:, :] = second_ref[...]


def one_hot(row, count):
    classes = lax.broadcasted_iota(jnp.int32, (HALO, count), 0)
    return (row.astype(jnp.int32) == classes).astype(F32)


def rows_of(hot, table):
    return lax.dot_general(
        hot, table, (((0,), (0,)), ((), ())), preferred_element_type=F32, precision=HIGHEST
    )


def near_strand_kernel(
    far_ref, weight_ref, values0_ref, grad_ref, tokens_ref, filter_ref, bias_ref,
    values1_ref, conv_grad_ref, mirror_ref, terms_ref,
):
    rows, width = grad_ref.shape[1], grad_ref.shape[2]
    taps = filter_ref.shape[0]
    values1_ref[...] = dot(reverse_both(far_ref[...]), weight_ref[...]).astype(BF16).astype(F32)
    hot = one_hot(tokens_ref[0], LANES)
    wide = 2 * LANES
    for index in range(width // wide):
        cols = slice(index * wide, (index + 1) * wide)
        weights = filter_ref[:, cols]
        own = grad_ref[0, :, cols].astype(F32)
        gate = jax.nn.sigmoid(values1_ref[:, cols] + rows_of(hot, bias_ref[:, cols]))
        conv_grad = own * gate
        conv_grad_ref[:, cols] = conv_grad
        conv = jnp.zeros((rows, wide), F32)
        for tap in range(taps):
            shifted = values0_ref[HALO - tap : HALO - tap + rows, cols]
            conv = conv + weights[tap : tap + 1] * shifted
            terms_ref[tap : tap + 1, cols] = jnp.sum(conv_grad * shifted, axis=0, keepdims=True)
        pre = own * conv * gate * (1.0 - gate)
        mirror_ref[:, cols] = pre.astype(BF16)
        terms_ref[8:16, cols] = jnp.dot(hot, pre, preferred_element_type=F32, precision=HIGHEST)
    terms_ref[7:8, :] = jnp.zeros((1, width), F32)


def far_strand_kernel(
    taps, slab_ref, weight_ref, values0_ref, values1_ref, mirror_ref, heads_ref,
    filter_rev_ref, bias_ref, bias_rev_ref,
    send_ref, mirror_out_ref, edge_ref,
    wide1, pull1, sums,
):
    rows, width = mirror_ref.shape
    tokens = slab_ref[HALO + rows :, :].astype(F32)[HALO - 1 : HALO, :]
    hot_own = one_hot(tokens[:, :LANES], LANES)
    hot_far = one_hot(tokens[:, LANES : 2 * LANES], LANES)
    hot_edge = one_hot(heads_ref[0].astype(F32)[HALO - 1 : HALO, :LANES], LANES)
    edge = dot(slab_ref[HALO + rows :, :], weight_ref[...]).astype(BF16).astype(F32)
    edge_gate = jax.nn.sigmoid(edge + rows_of(hot_edge, bias_ref[...])[0:HALO])
    edge_ref[...] = heads_ref[0].astype(F32) * edge_gate
    sums[...] = jnp.zeros_like(sums)
    wide = 2 * LANES
    for index in range(width // wide):
        cols = slice(index * wide, (index + 1) * wide)
        weights = filter_rev_ref[:, cols]
        wide1[0:rows, :] = values1_ref[:, cols]
        wide1[rows:, :] = edge[:, cols]
        own = slab_ref[HALO : HALO + rows, cols].astype(F32)
        gate = jax.nn.sigmoid(values0_ref[HALO:, cols] + rows_of(hot_own, bias_rev_ref[:, cols]))
        far_gate = jax.nn.sigmoid(
            values0_ref[0:HALO, cols] + rows_of(hot_far, bias_rev_ref[:, cols])[LANES - HALO :]
        )
        conv_grad = own * gate
        pull1[HALO:, :] = conv_grad
        pull1[0:HALO, :] = slab_ref[0:HALO, cols].astype(F32) * far_gate
        conv = jnp.zeros((rows, wide), F32)
        for tap in range(taps):
            shifted = wide1[tap : tap + rows, :]
            conv = conv + weights[tap : tap + 1] * shifted
            sums[tap : tap + 1, cols] = jnp.sum(conv_grad * shifted, axis=0, keepdims=True)
        pre = own * conv * gate * (1.0 - gate)
        mirror_out_ref[:, cols] = pre.astype(BF16)
        sums[8:16, cols] = jnp.dot(hot_own, pre, preferred_element_type=F32, precision=HIGHEST)
        total = mirror_ref[:, cols].astype(F32)
        for tap in range(taps):
            total = total + weights[tap : tap + 1] * pull1[HALO - tap : HALO - tap + rows, :]
        send_ref[0:rows, cols] = total.astype(BF16)
    send_ref[rows:, :] = sums[...].astype(BF16)


def operands_kernel(
    normed_ref, conv_grad_ref, edge_ref, mirror_ref, filter_ref, left_ref, right_ref, pull0,
):
    rows, width = conv_grad_ref.shape
    half = width // 2
    pull0[0:rows, :] = conv_grad_ref[...]
    pull0[rows:, :] = edge_ref[...]
    for strand in range(2):
        value = normed_ref[strand]
        left_ref[strand * rows : (strand + 1) * rows, :] = value[:, :half]
        left_ref[(2 + strand) * rows : (3 + strand) * rows, :] = reverse_both(value)[:, :half]
    wide = 2 * LANES
    for index in range(width // wide):
        cols = slice(index * wide, (index + 1) * wide)
        total = mirror_ref[:, cols].astype(F32)
        for tap in range(filter_ref.shape[0]):
            total = total + filter_ref[tap : tap + 1, cols] * pull0[tap : tap + rows, cols]
        right_ref[0:rows, cols] = total.astype(BF16)
    right_ref[rows:, :] = reverse_both(right_ref[0:rows, :])


def project_kernel(
    place_ref, scale, left_ref, right_ref, back_ref, terms_ref,
    send_ref, keep_ref, sums_ref, final_ref,
):
    rows = right_ref.shape[0] // 2
    back = back_ref[0:rows, :]
    home = reverse_both(back)
    final_ref[0] = right_ref[0:rows, :]
    final_ref[1] = home
    right = jnp.concatenate([right_ref[0:rows, :], home, right_ref[rows:, :], back], axis=0)
    sums = (terms_ref[...] + reverse_lanes(back_ref[rows:, :]).astype(F32)) * scale
    sums_ref[...] = sums
    core = place_ref[0] % 2
    shard = left_ref.shape[1] // 4
    for chip in range(2):
        for mine in range(2):
            index = chip * 2 + (core if mine else 1 - core)
            left = left_ref[:, pl.ds(pl.multiple_of(index * shard, shard), shard)]
            part = lax.dot_general(left, right, (((0,), (0,)), ((), ())), preferred_element_type=F32) * scale
            if mine:
                keep_ref[chip * shard : (chip + 1) * shard, :] = part
            else:
                send_ref[chip * shard : (chip + 1) * shard, :] = part.astype(BF16)
    send_ref[2 * shard :, :] = sums.astype(BF16)


def input_grad_kernel(value_grad_ref, weight_ref, out_ref):
    weight = weight_ref[...]
    for strand in range(2):
        out_ref[strand] = lax.dot_general(
            value_grad_ref[strand], weight, (((1,), (1,)), ((), ())), preferred_element_type=F32
        ).astype(BF16)


def first_sum_kernel(place_ref, keep_ref, got_ref, sums_ref, send_ref, keep_out_ref, sums_out_ref):
    shard = keep_ref.shape[0] // 2
    x_lo = place_ref[0] // 2
    here = pl.ds(pl.multiple_of(x_lo * shard, shard), shard)
    there = pl.ds(pl.multiple_of((1 - x_lo) * shard, shard), shard)
    keep_out_ref[...] = keep_ref[here, :] + got_ref[here, :].astype(F32)
    send_ref[0:shard, :] = (keep_ref[there, :] + got_ref[there, :].astype(F32)).astype(BF16)
    sums = sums_ref[...] + got_ref[2 * shard :, :].astype(F32)
    sums_out_ref[...] = sums
    send_ref[shard:, :] = sums.astype(BF16)


def last_sum_kernel(place_ref, keep_ref, got_ref, sums_ref, proj_ref, filter_ref, bias_ref):
    shard = keep_ref.shape[0]
    part = filter_ref.shape[2]
    proj_ref[...] = keep_ref[...] + got_ref[0:shard, :].astype(F32)
    cols = pl.ds(pl.multiple_of(place_ref[0] * part, part), part)
    sums = sums_ref[:, cols] + got_ref[shard:, cols].astype(F32)
    for tap in range(filter_ref.shape[0]):
        filter_ref[tap] = sums[tap : tap + 1, :]
    for token in range(bias_ref.shape[0]):
        bias_ref[token] = sums[8 + token : 9 + token, :]


def mirrored(value):
    size = lax.axis_size("ctx")
    return lax.ppermute(value, "ctx", [(i, size - 1 - i) for i in range(size)])


def shifted(value, distance):
    size = lax.axis_size("ctx")
    middle = {size // 2 - 1, size // 2}
    pairs = [(i, i + distance) for i in range(size) if 0 <= i + distance < size and {i, i + distance} != middle]
    return lax.ppermute(value, "ctx", pairs)


def partner(value, bit):
    return lax.ppermute(value, "fsdp", [(i, i ^ bit) for i in range(lax.axis_size("fsdp"))])


def shape(dims, dtype):
    return jax.ShapeDtypeStruct(dims, dtype)


def step(normed, out_grad, ids, mask, proj_half, conv_filter, gate_bias):
    rows, width = normed.shape[2], normed.shape[3]
    taps = conv_filter.shape[0]
    shard = proj_half.shape[0]
    classes = gate_bias.shape[0]
    normed, out_grad = normed[:, 0], out_grad[:, 0]
    place = lax.axis_index("fsdp").astype(jnp.int32).reshape(1)

    send, tails, heads, far_grad, tokens, rims = pl.pallas_call(
        lead_kernel,
        out_shape=(
            shape((rows, width), BF16),
            shape((2, HALO, width), BF16),
            shape((2, HALO, width), BF16),
            shape((rows, width), BF16),
            shape((2, 1, rows), F32),
            shape((4, HALO, width), BF16),
        ),
        in_specs=[pl.BlockSpec(memory_space=pltpu.HBM)] * 4,
        out_specs=[pl.BlockSpec(memory_space=pltpu.VMEM)] * 6,
        scratch_shapes=[
            pltpu.VMEM((2, HALO, width), BF16),
            pltpu.VMEM((2, 1, rows), jnp.int32),
            pltpu.VMEM((2, 1, rows), jnp.int32),
            pltpu.SemaphoreType.DMA((6,)),
        ],
        cost_estimate=pl.CostEstimate(flops=0, bytes_accessed=4 * rows * width, transcendentals=0),
    )(normed, out_grad, ids, mask)
    middle = lax.axis_size("ctx") // 2
    shard_index = lax.axis_index("ctx").astype(jnp.int32).reshape(1)
    rims = lax.ppermute(rims, "ctx", [(middle - 1, middle), (middle, middle - 1)])
    normed_far = mirrored(send)
    heads = shifted(heads, -1)
    tails = shifted(tails, 1)
    near = partner(proj_half, 2)
    slab, tails, heads = call(
        functools.partial(pack_kernel, middle),
        (shape((rows + 2 * HALO, width), BF16), shape((2, HALO, width), BF16), shape((2, HALO, width), BF16)),
        shard_index, far_grad, tokens, tails, heads, rims, scalars=1,
        flops=600 * rows * width, moved=4 * rows * width,
    )
    slab = mirrored(slab)
    pair, = call(join_kernel, (shape((2 * shard, width), BF16),), proj_half, near, moved=8 * shard * width)
    other = partner(pair, 1)
    weight, values0, filter_rev, bias, bias_rev = call(
        forward_kernel,
        (shape((width, width), BF16), shape((rows + HALO, width), F32)) + (shape((HALO, width), F32),) * 3,
        place, proj_half, near, other, normed, tails, conv_filter, gate_bias, scalars=1,
        flops=2 * rows * width * width, moved=6 * width * width,
    )
    values1, conv_grad, mirror0, terms = call(
        near_strand_kernel,
        (
            shape((rows, width), F32),
            shape((rows, width), F32),
            shape((rows, width), BF16),
            shape((16, width), F32),
        ),
        normed_far, weight, values0, out_grad, tokens, conv_filter, bias,
        flops=2 * rows * width * width, moved=8 * width * width,
    )
    wide = 2 * LANES
    send, mirror1, edge = call(
        functools.partial(far_strand_kernel, taps),
        (shape((rows + 16, width), BF16), shape((rows, width), BF16), shape((HALO, width), F32)),
        slab, weight, values0, values1, mirror0, heads, filter_rev, bias, bias_rev,
        scratch=[pltpu.VMEM((rows + HALO, wide), F32)] * 2 + [pltpu.VMEM((16, width), F32)],
        flops=2 * rows * width * width, moved=8 * width * width,
    )
    back = mirrored(send)
    left, right = call(
        operands_kernel, (shape((4 * rows, width // 2), BF16), shape((2 * rows, width), BF16)),
        normed, conv_grad, edge, mirror1, conv_filter,
        scratch=[pltpu.VMEM((rows + HALO, width), F32)],
        flops=rows * width * width, moved=16 * rows * width,
    )
    grad_scale = 1.0 / math.sqrt(2.0 * lax.axis_size("fsdp") * rows)
    send1, keep1, sums1, final = call(
        lambda place_ref, *refs: project_kernel(place_ref, grad_scale, *refs),
        (
            shape((2 * shard + 16, width), BF16),
            shape((2 * shard, width), F32),
            shape((16, width), F32),
            shape((2, rows, width), BF16),
        ),
        place, left, right, back, terms, scalars=1,
        flops=4 * rows * width * width, moved=4 * width * width,
    )
    got1 = partner(send1, 1)
    send2, keep2, sums2 = call(
        first_sum_kernel,
        (shape((shard + 16, width), BF16), shape((shard, width), F32), shape((16, width), F32)),
        place, keep1, got1, sums1, scalars=1, moved=16 * shard * width,
    )
    got2 = partner(send2, 2)
    in_grad, = call(
        input_grad_kernel, (shape((2, rows, width), BF16),), final, weight,
        flops=4 * rows * width * width, moved=4 * width * width,
    )
    part = width // lax.axis_size("fsdp")
    proj_grad, filter_grad, bias_grad = call(
        last_sum_kernel,
        (shape((shard, width), F32), shape((taps, 1, part), F32), shape((classes, 1, part), F32)),
        place, keep2, got2, sums2, scalars=1, moved=12 * shard * width,
    )
    return (
        in_grad[:, None],
        proj_grad[None],
        jnp.transpose(filter_grad, (1, 0, 2)),
        jnp.transpose(bias_grad, (1, 0, 2)),
    )


def solution(mesh):
    placed = (
        P(None, "fsdp", "ctx", None),
        P(None, "fsdp", "ctx", None),
        P(None, "fsdp", "ctx"),
        P(None, "fsdp", "ctx"),
        P("fsdp", None),
        P(),
        P(),
    )
    return jax.shard_map(
        step,
        mesh=mesh,
        in_specs=placed,
        out_specs=(
            P(None, "fsdp", "ctx", None),
            P("ctx", "fsdp", None),
            P("ctx", None, "fsdp"),
            P("ctx", None, "fsdp"),
        ),
        check_vma=False,
    )
```
